256 devices in a mesh: row: 16 (over z, core), col: 16 (over y, x).
Axes of the slice: x: 4, y: 4, z: 8, core: 2. Of those that a mesh axis runs over, the one named last changes fastest.
Arguments:
- points: float32 [32, 65536], P(None, ('row', 'col')), may hold values from -6 to 6
- search: float32 [96, 65536], P(None, ('row', 'col')), may hold values from -24 to 24
Outputs:
- applied: float32 [96, 65536], P(None, ('row', 'col'))
- gram_a: float32 [96, 96], replicated
- gram_b: float32 [96, 96], replicated
- q_block: float32 [32, 65536], P(None, ('row', 'col'))
The draws below stay inside these ranges and needn't reach their ends.
All inputs are finite; a program needn't handle non-finite values.
Results may differ from the reference program's by a relative error of at most 0.00036.
Values may be sent and summed in bfloat16 or wider, within the bound.
A program may use at most 128 MiB of HBM per device.

```python
import math
import jax
import jax.numpy as jnp
from jax import lax

DIM = 32
NEV = 32
BLOCK = 96
N = 65536


def shared_draw(key):
    draw_key = jax.random.fold_in(key, 101)
    positions = jnp.arange(N, dtype=jnp.float32) / N
    points = jnp.clip(jax.random.normal(draw_key, (DIM, N), jnp.float32), -6.0, 6.0)
    growth = 3.0 ** positions
    perturb = 0.5 * jax.random.normal(jax.random.fold_in(key, 102), (3 * NEV, N), jnp.float32) * growth[None, :]
    mixing = jax.random.normal(jax.random.fold_in(key, 103), (NEV, DIM), jnp.float32) / math.sqrt(DIM)
    iterates = points[:NEV] + perturb[:NEV]
    residuals = 0.7 * (points[:NEV] * points[:NEV] - 1.0) + perturb[NEV:2 * NEV]
    directions = jnp.dot(mixing, points) + perturb[2 * NEV:]
    search = jnp.clip(jnp.concatenate([iterates, residuals, directions], axis=0), -24.0, 24.0)
    return (points, search)


def draw_points(key, part):
    return shared_draw(key)[0]


def draw_search(key, part):
    return shared_draw(key)[1]


def setup_inputs(seed: int = 0) -> dict:
    keys = jax.random.split(jax.random.key(seed), 3)
    return {
        "points": draw_points(jax.random.fold_in(keys[2], 71), 0),
        "search": draw_search(jax.random.fold_in(keys[2], 71), 0),
    }


def affinity_rows(target_points, target_squares, points, squares, kernel_rate):
    cross_terms = jnp.dot(target_points.T.astype(jnp.float32), points.astype(jnp.float32), precision=lax.Precision.HIGHEST, preferred_element_type=jnp.float32)
    distances = target_squares[:, None] + squares[None, :] - 2.0 * cross_terms
    return jnp.exp(-kernel_rate * distances)

def reference(points, search):
    kernel_rate = 2.0 / DIM
    squares = lax.optimization_barrier(jnp.sum(points * points, axis=0))
    rows_block = math.gcd(N, 1024)
    block_count = N // rows_block
    target_points = points.reshape(DIM, block_count, rows_block).transpose(1, 0, 2)
    target_squares = squares.reshape(block_count, rows_block)

    def degree_rows(pair):
        return lax.optimization_barrier(jnp.sum(affinity_rows(pair[0], pair[1], points, squares, kernel_rate), axis=1))
    degrees = lax.map(degree_rows, (target_points, target_squares)).reshape(N)
    inverse_root = lax.rsqrt(degrees)
    scaled = (search * inverse_root[None, :]).astype(jnp.bfloat16)

    def image_rows(pair):
        affinity = affinity_rows(pair[0], pair[1], points, squares, kernel_rate).astype(jnp.bfloat16)
        return jnp.dot(scaled.astype(jnp.float32), affinity.T.astype(jnp.float32), preferred_element_type=jnp.float32)
    blocks = lax.map(image_rows, (target_points, target_squares))
    applied = blocks.transpose(1, 0, 2).reshape(BLOCK, N) * inverse_root[None, :]
    gram_a = jnp.dot(search, applied.T, precision=lax.Precision.HIGHEST) / N
    gram_b = jnp.dot(search, search.T, precision=lax.Precision.HIGHEST) / N
    factor_b = jnp.linalg.cholesky(gram_b[:NEV, :NEV])
    mapping = jax.scipy.linalg.cho_solve((factor_b, True), gram_a[:NEV, :NEV]).T
    residual = applied[:NEV] - jnp.dot(mapping, search[:NEV], precision=lax.Precision.HIGHEST)
    residual_gram = jnp.dot(residual, residual.T, precision=lax.Precision.HIGHEST) / N
    factor_r = jnp.linalg.cholesky(residual_gram)
    q_block = jax.scipy.linalg.solve_triangular(factor_r, residual, lower=True)
    return (applied, gram_a, gram_b, q_block)
```

```python
import functools
import math

import jax
import jax.numpy as jnp
from jax import lax
from jax.experimental import pallas as pl
from jax.experimental.pallas import tpu as pltpu
from jax.sharding import PartitionSpec as P

NEV = 32
MESH = pl.DeviceIdType.MESH
HIGH = lax.Precision.HIGHEST
DEPTH = 256
LANES = 128


def contract(a, b, dims):
    return lax.dot_general(
        a, b, (dims, ((), ())), precision=HIGH, preferred_element_type=jnp.float32
    )


def split3(x):
    hi = x.astype(jnp.bfloat16)
    rest = x - hi.astype(jnp.float32)
    mid = rest.astype(jnp.bfloat16)
    low = (rest - mid.astype(jnp.float32)).astype(jnp.bfloat16)
    return hi, mid, low


def lifted(x, rate, is_source):
    dim, n = x.shape
    squares = jnp.broadcast_to(-rate * jnp.sum(x * x, axis=0, keepdims=True), (16, n))
    row = lax.broadcasted_iota(jnp.int32, (16, n), 0)
    parts = split3(squares)
    one = jnp.ones((16, n), jnp.float32)
    first = jnp.where(row == 0, parts[0].astype(jnp.float32), 0.0)
    first = jnp.where(row == 1, parts[1].astype(jnp.float32), first)
    first = jnp.where(row == 2, parts[2].astype(jnp.float32), first)
    second = jnp.where(row < 3, one, 0.0)
    if is_source:
        hi, mid, low = split3(x)
        blocks = [hi, hi, mid, hi, low, mid]
        extra = [first, second]
    else:
        hi, mid, low = split3(x * (2.0 * rate))
        blocks = [hi, mid, hi, low, hi, mid]
        extra = [second, first]
    blocks = blocks + [e.astype(jnp.bfloat16) for e in extra]
    used = 6 * dim + 32
    if used < DEPTH:
        blocks.append(jnp.zeros((DEPTH - used, n), jnp.bfloat16))
    return jnp.concatenate(blocks, axis=0)


def inverse_factor(gram):
    k = gram.shape[0]
    row = lax.broadcasted_iota(jnp.int32, (k, k), 0)
    col = lax.broadcasted_iota(jnp.int32, (k, k), 1)
    eye = jnp.where(row == col, 1.0, 0.0)
    pad = jnp.zeros((k, LANES - 2 * k), jnp.float32)
    work = jnp.concatenate([gram, eye, pad], axis=1)
    below = lax.broadcasted_iota(jnp.int32, (k, 1), 0)
    for step in range(k):
        pivot_row = work[step : step + 1, :]
        pivot = work[step : step + 1, step : step + 1]
        factor = jnp.where(below > step, work[:, step : step + 1] / pivot, 0.0)
        work = work - factor * pivot_row
    diagonal = jnp.sum(work[:, :k] * eye, axis=1, keepdims=True)
    return work[:, k : 2 * k] * lax.rsqrt(diagonal)


def pack(square):
    return jnp.concatenate([square[8 * i : 8 * i + 8, :] for i in range(4)], axis=1)


def unpack(flat):
    return jnp.concatenate([flat[:, 32 * i : 32 * i + 32] for i in range(4)], axis=0)


def kernel(
    R, C, n, points_ref, search_ref, applied_ref, gram_a_ref, gram_b_ref, q_ref,
    src_pts, tgt_pts, tgt_lift, tile, deg, deg_in, scal, outp, out_in,
    a_part, a_in, a_piece, a_in2, a_res,
    b_part, b_in, b_piece, b_in2, b_res,
    x_part, x_in, x_piece, x_in2,
    y_part, y_in, y_piece, y_in2,
    ssem, rsem,
):
    r = lax.axis_index("row")
    c = lax.axis_index("col")
    total = R * C * n
    rate = (2.0 / points_ref.shape[0]) * math.log2(math.e)
    Z = R // 2

    def along_row(d):
        return lax.rem(r + d, R)

    def along_col(d):
        return lax.rem(c + d, C)

    def row_copy(phase, src, dst, peer, slot):
        return pltpu.make_async_remote_copy(
            src_ref=src, dst_ref=dst, send_sem=ssem.at[phase, peer], recv_sem=rsem.at[phase, slot],
            device_id=(peer, c), device_id_type=MESH,
        )

    def col_copy(phase, src, dst, peer, slot):
        return pltpu.make_async_remote_copy(
            src_ref=src, dst_ref=dst, send_sem=ssem.at[phase, peer], recv_sem=rsem.at[phase, slot],
            device_id=(r, peer), device_id_type=MESH,
        )

    def row_all(phase, src_of, dst, what):
        def body(d, _):
            peer = along_row(d)
            if what == "start":
                row_copy(phase, src_of(peer), dst.at[r], peer, r).start()
            elif what == "recv":
                row_copy(phase, src_of(peer), dst.at[peer], peer, peer).wait_recv()
            else:
                row_copy(phase, src_of(peer), dst.at[r], peer, r).wait_send()
            return 0

        lax.fori_loop(1, R, body, 0)

    def col_all(phase, src_of, dst, what):
        def body(d, _):
            peer = along_col(d)
            if what == "start":
                col_copy(phase, src_of(peer), dst.at[c], peer, c).start()
            elif what == "recv":
                col_copy(phase, src_of(peer), dst.at[peer], peer, peer).wait_recv()
            else:
                col_copy(phase, src_of(peer), dst.at[c], peer, c).wait_send()
            return 0

        lax.fori_loop(1, C, body, 0)

    barrier = pltpu.get_barrier_semaphore()

    def greet_row(d, _):
        pl.semaphore_signal(barrier, inc=1, device_id=(along_row(d), c), device_id_type=MESH)
        return 0

    def greet_col(d, _):
        pl.semaphore_signal(barrier, inc=1, device_id=(r, along_col(d)), device_id_type=MESH)
        return 0

    lax.fori_loop(1, R, greet_row, 0)
    lax.fori_loop(1, C, greet_col, 0)
    pl.semaphore_wait(barrier, R + C - 2)

    TGT, SRC, DEG, SCAL, OUT, B1, B2, B3, A1, A2, A3, X1, X2, Y1, Y2 = range(15)
    my_points = lambda peer: points_ref
    col_all(TGT, my_points, tgt_pts, "start")
    row_all(SRC, my_points, src_pts, "start")
    src_pts[r] = points_ref[...]
    tgt_pts[c] = points_ref[...]

    rows = 96
    piece = LANES // R

    def stage_square(part, square):
        wide = jnp.concatenate([square, jnp.zeros((rows, LANES - rows), jnp.float32)], axis=1)
        for i in range(R):
            if (i + 1) * piece <= rows:
                part[i] = wide[i * piece : (i + 1) * piece]
            else:
                live = max(0, rows - i * piece)
                rest = jnp.zeros((piece - live, LANES), jnp.float32)
                part[i] = jnp.concatenate([wide[i * piece : i * piece + live], rest], axis=0) if live else rest

    def round1(phase, part, inbox):
        row_all(phase, lambda peer: part.at[peer], inbox, "start")
        inbox[r] = part[r]

    def round2(phase, part, inbox, piece_ref, inbox2):
        row_all(phase, lambda peer: part.at[peer], inbox, "recv")
        value = inbox[0]
        for i in range(1, R):
            value = value + inbox[i]
        piece_ref[0] = value
        col_all(phase + 1, lambda peer: piece_ref.at[0], inbox2, "start")
        inbox2[c] = value

    def round3(phase, piece_ref, inbox2, result):
        col_all(phase + 1, lambda peer: piece_ref.at[0], inbox2, "recv")
        value = inbox2[0]
        for i in range(1, C):
            value = value + inbox2[i]
        piece_ref[1] = value * (1.0 / total)
        row_all(phase + 2, lambda peer: piece_ref.at[1], result, "start")
        result[r] = value * (1.0 / total)

    def finish(phase, piece_ref, result):
        row_all(phase + 2, lambda peer: piece_ref.at[1], result, "recv")
        square = jnp.concatenate([result[i] for i in range(R)], axis=0)
        return square[:rows, :rows]

    def drain(phase, part, inbox, piece_ref, inbox2, result):
        row_all(phase, lambda peer: part.at[peer], inbox, "send")
        col_all(phase + 1, lambda peer: piece_ref.at[0], inbox2, "send")
        if result is not None:
            row_all(phase + 2, lambda peer: piece_ref.at[1], result, "send")

    def small_sum(phase, square, part, inbox, piece_ref, inbox2):
        flat = pack(square)
        part[0] = flat
        row_all(phase, lambda peer: part.at[0], inbox, "start")
        inbox[r] = flat
        row_all(phase, lambda peer: part.at[0], inbox, "recv")
        value = inbox[0]
        for i in range(1, R):
            value = value + inbox[i]
        piece_ref[0] = value
        col_all(phase + 1, lambda peer: piece_ref.at[0], inbox2, "start")
        inbox2[c] = value
        col_all(phase + 1, lambda peer: piece_ref.at[0], inbox2, "recv")
        value = inbox2[0]
        for i in range(1, C):
            value = value + inbox2[i]
        return unpack(value) * (1.0 / total)

    search = search_ref[...]
    stage_square(b_part, contract(search, search, ((1,), (1,))))
    round1(B1, b_part, b_in)

    def lift_target(d, _):
        peer = along_col(d)

        @pl.when(d > 0)
        def _():
            col_copy(TGT, points_ref, tgt_pts.at[peer], peer, peer).wait_recv()

        tgt_lift[:, pl.ds(pl.multiple_of(peer * n, n), n)] = lifted(tgt_pts[peer], rate, False)
        return 0

    lax.fori_loop(0, C, lift_target, 0)
    round2(B1, b_part, b_in, b_piece, b_in2)

    deg[...] = jnp.zeros_like(deg)
    z0 = r // 2
    core0 = lax.rem(r, 2)

    def nearest(i):
        k = i // 2
        half = (k + 1) // 2
        delta = jnp.where(lax.rem(k, 2) == 1, half, Z - half)
        z = lax.rem(z0 + delta, Z)
        return z * 2 + lax.rem(core0 + i, 2)

    def affinities(i, _):
        peer = nearest(i)

        @pl.when(i > 0)
        def _():
            row_copy(SRC, points_ref, src_pts.at[peer], peer, peer).wait_recv()

        sources = lifted(src_pts[peer], rate, True)
        exponent = lax.dot_general(
            sources, tgt_lift[...], (((0,), (0,)), ((), ())), preferred_element_type=jnp.float32
        )
        affinity = jnp.exp2(exponent)
        deg[...] += jnp.sum(affinity.reshape(n // 8, 8, C * n), axis=0)
        tile[pl.ds(pl.multiple_of(peer * n, n), n), :] = affinity.astype(jnp.bfloat16)
        return 0

    lax.fori_loop(0, R, affinities, 0)

    window = lambda peer: deg.at[:, pl.ds(pl.multiple_of(peer * n, n), n)]
    col_all(DEG, window, deg_in, "start")
    deg_in[c] = deg[:, pl.ds(pl.multiple_of(c * n, n), n)]
    round3(B1, b_piece, b_in2, b_res)
    col_all(DEG, window, deg_in, "recv")
    sums = deg_in[0]
    for i in range(1, C):
        sums = sums + deg_in[i]
    degrees = jnp.sum(sums, axis=0, keepdims=True)
    root = lax.rsqrt(degrees)
    root = root * (1.5 - 0.5 * degrees * root * root)
    scal[r] = (search_ref[...] * root).astype(jnp.bfloat16)
    row_all(SCAL, lambda peer: scal.at[r], scal, "start")

    gram_b = finish(B1, b_piece, b_res)
    gram_b_ref[...] = gram_b
    factor = inverse_factor(gram_b[:NEV, :NEV])
    solved = contract(factor, contract(factor, search_ref[:NEV, :], ((1,), (0,))), ((0,), (0,)))

    row_all(SCAL, lambda peer: scal.at[r], scal, "recv")
    pairs = C // 2
    pair0 = c // 2

    def images(j, _):
        pair = lax.rem(pair0 + 1 + j, pairs)
        at = pl.ds(pl.multiple_of(pair * (2 * n), 2 * n), 2 * n)
        value = jnp.dot(scal[0], tile[0:n, at], preferred_element_type=jnp.float32)
        for i in range(1, R):
            value = value + jnp.dot(
                scal[i], tile[i * n : (i + 1) * n, at], preferred_element_type=jnp.float32
            )
        for half in range(2):
            peer = pair * 2 + half
            outp[peer] = value[:, half * n : (half + 1) * n]

            @pl.when(peer != c)
            def _():
                col_copy(OUT, outp.at[peer], out_in.at[c], peer, c).start()

        return 0

    lax.fori_loop(0, pairs, images, 0)
    out_in[c] = outp[c]
    col_all(OUT, lambda peer: outp.at[peer], out_in, "recv")
    sums = out_in[0]
    for i in range(1, C):
        sums = sums + out_in[i]
    applied = sums * root
    applied_ref[...] = applied

    local_a = contract(search_ref[...], applied, ((1,), (1,)))
    stage_square(a_part, local_a)
    round1(A1, a_part, a_in)
    leading = small_sum(X1, local_a[:NEV, :NEV], x_part, x_in, x_piece, x_in2)
    residual = applied[:NEV] - contract(leading, solved, ((0,), (0,)))
    local_r = contract(residual, residual, ((1,), (1,)))
    round2(A1, a_part, a_in, a_piece, a_in2)
    residual_gram = small_sum(Y1, local_r, y_part, y_in, y_piece, y_in2)
    round3(A1, a_piece, a_in2, a_res)
    q_ref[...] = contract(inverse_factor(residual_gram), residual, ((1,), (0,)))
    gram_a_ref[...] = finish(A1, a_piece, a_res)

    col_all(TGT, my_points, tgt_pts, "send")
    row_all(SRC, my_points, src_pts, "send")
    col_all(DEG, window, deg_in, "send")
    row_all(SCAL, lambda peer: scal.at[r], scal, "send")
    col_all(OUT, lambda peer: outp.at[peer], out_in, "send")
    drain(B1, b_part, b_in, b_piece, b_in2, b_res)
    drain(A1, a_part, a_in, a_piece, a_in2, a_res)
    for phase, part, inbox, piece_ref, inbox2 in (
        (X1, x_part, x_in, x_piece, x_in2),
        (Y1, y_part, y_in, y_piece, y_in2),
    ):
        row_all(phase, lambda peer: part.at[0], inbox, "send")
        col_all(phase + 1, lambda peer: piece_ref.at[0], inbox2, "send")


def per_device(R, C, points, search):
    dim, n = points.shape
    rows = search.shape[0]
    f32 = jnp.float32
    piece = LANES // R
    square = lambda: [
        pltpu.VMEM((R, piece, LANES), f32),
        pltpu.VMEM((R, piece, LANES), f32),
        pltpu.VMEM((2, piece, LANES), f32),
        pltpu.VMEM((C, piece, LANES), f32),
        pltpu.VMEM((R, piece, LANES), f32),
    ]
    small = lambda: [
        pltpu.VMEM((1, 8, LANES), f32),
        pltpu.VMEM((R, 8, LANES), f32),
        pltpu.VMEM((1, 8, LANES), f32),
        pltpu.VMEM((C, 8, LANES), f32),
    ]
    vmem = pl.BlockSpec(memory_space=pltpu.VMEM)
    most = max(R, C)
    return pl.pallas_call(
        functools.partial(kernel, R, C, n),
        out_shape=(
            jax.ShapeDtypeStruct((rows, n), f32),
            jax.ShapeDtypeStruct((rows, rows), f32),
            jax.ShapeDtypeStruct((rows, rows), f32),
            jax.ShapeDtypeStruct((NEV, n), f32),
        ),
        in_specs=[vmem, vmem],
        out_specs=(vmem, vmem, vmem, vmem),
        scratch_shapes=[
            pltpu.VMEM((R, dim, n), f32),
            pltpu.VMEM((C, dim, n), f32),
            pltpu.VMEM((DEPTH, C * n), jnp.bfloat16),
            pltpu.VMEM((R * n, C * n), jnp.bfloat16),
            pltpu.VMEM((8, C * n), f32),
            pltpu.VMEM((C, 8, n), f32),
            pltpu.VMEM((R, rows, n), jnp.bfloat16),
            pltpu.VMEM((C, rows, n), f32),
            pltpu.VMEM((C, rows, n), f32),
            *square(),
            *square(),
            *small(),
            *small(),
            pltpu.SemaphoreType.DMA((15, most)),
            pltpu.SemaphoreType.DMA((15, most)),
        ],
        compiler_params=pltpu.CompilerParams(
            collective_id=0, has_side_effects=True, vmem_limit_bytes=60 << 20
        ),
    )(points, search)


def solution(mesh):
    placed = (P(None, ("row", "col")), P(None, ("row", "col")))
    return jax.shard_map(
        functools.partial(per_device, mesh.shape["row"], mesh.shape["col"]),
        mesh=mesh,
        in_specs=placed,
        out_specs=(P(None, ("row", "col")), P(), P(), P(None, ("row", "col"))),
        check_vma=False,
    )
```

```python
import functools
import math

import jax
import jax.numpy as jnp
from jax import lax
from jax.experimental import pallas as pl
from jax.experimental.pallas import tpu as pltpu
from jax.sharding import PartitionSpec as P

NEV = 32
MESH = pl.DeviceIdType.MESH
HIGH = lax.Precision.HIGHEST
DEPTH = 256
LANES = 128


def contract(a, b, dims):
    return lax.dot_general(
        a, b, (dims, ((), ())), precision=HIGH, preferred_element_type=jnp.float32
    )


def split3(x):
    hi = x.astype(jnp.bfloat16)
    rest = x - hi.astype(jnp.float32)
    mid = rest.astype(jnp.bfloat16)
    low = (rest - mid.astype(jnp.float32)).astype(jnp.bfloat16)
    return hi, mid, low


def lifted(x, rate, is_source):
    dim, n = x.shape
    squares = jnp.broadcast_to(-rate * jnp.sum(x * x, axis=0, keepdims=True), (16, n))
    row = lax.broadcasted_iota(jnp.int32, (16, n), 0)
    parts = split3(squares)
    one = jnp.ones((16, n), jnp.float32)
    first = jnp.where(row == 0, parts[0].astype(jnp.float32), 0.0)
    first = jnp.where(row == 1, parts[1].astype(jnp.float32), first)
    first = jnp.where(row == 2, parts[2].astype(jnp.float32), first)
    second = jnp.where(row < 3, one, 0.0)
    if is_source:
        hi, mid, low = split3(x)
        blocks = [hi, hi, mid, hi, low, mid]
        extra = [first, second]
    else:
        hi, mid, low = split3(x * (2.0 * rate))
        blocks = [hi, mid, hi, low, hi, mid]
        extra = [second, first]
    blocks = blocks + [e.astype(jnp.bfloat16) for e in extra]
    used = 6 * dim + 32
    if used < DEPTH:
        blocks.append(jnp.zeros((DEPTH - used, n), jnp.bfloat16))
    return jnp.concatenate(blocks, axis=0)


def inverse_factor(gram):
    k = gram.shape[0]
    row = lax.broadcasted_iota(jnp.int32, (k, k), 0)
    col = lax.broadcasted_iota(jnp.int32, (k, k), 1)
    eye = jnp.where(row == col, 1.0, 0.0)
    pad = jnp.zeros((k, LANES - 2 * k), jnp.float32)
    work = jnp.concatenate([gram, eye, pad], axis=1)
    below = lax.broadcasted_iota(jnp.int32, (k, 1), 0)
    for step in range(k):
        pivot_row = work[step : step + 1, :]
        pivot = work[step : step + 1, step : step + 1]
        factor = jnp.where(below > step, work[:, step : step + 1] / pivot, 0.0)
        work = work - factor * pivot_row
    diagonal = jnp.sum(work[:, :k] * eye, axis=1, keepdims=True)
    return work[:, k : 2 * k] * lax.rsqrt(diagonal)


def pack(square):
    return jnp.concatenate([square[8 * i : 8 * i + 8, :] for i in range(4)], axis=1)


def unpack(flat):
    return jnp.concatenate([flat[:, 32 * i : 32 * i + 32] for i in range(4)], axis=0)


def kernel(
    R, C, n, points_ref, search_ref, applied_ref, gram_a_ref, gram_b_ref, q_ref,
    src_pts, tgt_pts, tgt_lift, tile, deg, deg_in, scal, outp, out_in,
    a_part, a_in, a_piece, a_in2, a_res,
    b_part, b_in, b_piece, b_in2, b_res,
    x_part, x_in, x_piece, x_in2, image,
    ssem, rsem,
):
    r = lax.axis_index("row")
    c = lax.axis_index("col")
    total = R * C * n
    rate = (2.0 / points_ref.shape[0]) * math.log2(math.e)

    def along_row(d):
        return lax.rem(r + d, R)

    def along_col(d):
        return lax.rem(c + d, C)

    def row_copy(phase, src, dst, peer, slot):
        return pltpu.make_async_remote_copy(
            src_ref=src, dst_ref=dst, send_sem=ssem.at[phase, peer], recv_sem=rsem.at[phase, slot],
            device_id=(peer, c), device_id_type=MESH,
        )

    def col_copy(phase, src, dst, peer, slot):
        return pltpu.make_async_remote_copy(
            src_ref=src, dst_ref=dst, send_sem=ssem.at[phase, peer], recv_sem=rsem.at[phase, slot],
            device_id=(r, peer), device_id_type=MESH,
        )

    open_ends = {}

    def every(copy, me, size, phase, src_of, dst, what):
        def body(d, _):
            peer = lax.rem(me + d, size)
            if what == "start":
                copy(phase, src_of(peer), dst.at[me], peer, me).start()
            elif what == "recv":
                copy(phase, src_of(peer), dst.at[peer], peer, peer).wait_recv()
            else:
                copy(phase, src_of(peer), dst.at[me], peer, me).wait_send()
            return 0

        if what == "start":
            for end in ("recv", "send"):
                open_ends[phase, end] = functools.partial(
                    every, copy, me, size, phase, src_of, dst, end
                )
        else:
            del open_ends[phase, what]
        lax.fori_loop(1, size, body, 0)

    row_all = functools.partial(every, row_copy, r, R)
    col_all = functools.partial(every, col_copy, c, C)

    Z = R // 2
    z0, core0 = r // 2, lax.rem(r, 2)
    partner = z0 * 2 + 1 - core0

    def nearest(i):
        half = (i + 1) // 2
        return lax.rem(z0 + jnp.where(lax.rem(i, 2) == 1, half, Z - half), Z)

    class Spread:
        def __init__(self, direct, handed, buffer):
            self.direct, self.handed, self.buffer = direct, handed, buffer

        def direct_copy(self, src, peer, slot):
            return row_copy(self.direct, src, self.buffer.at[slot], peer, slot)

        def handed_copy(self, src, slot):
            return pltpu.make_async_remote_copy(
                src_ref=src, dst_ref=self.buffer.at[slot], send_sem=ssem.at[self.handed, slot],
                recv_sem=rsem.at[self.handed, slot], device_id=(partner, c), device_id_type=MESH,
            )

        def start(self, src):
            self.src = src

            def body(i, _):
                self.direct_copy(src, nearest(i) * 2 + core0, r).start()
                return 0

            self.handed_copy(src, r).start()
            lax.fori_loop(1, Z, body, 0)
            open_ends[self.direct, "send"] = self.sent

        def take(self, i):
            slot = nearest(i) * 2 + core0

            @pl.when(i > 0)
            def _():
                self.direct_copy(self.src, slot, slot).wait_recv()
                self.handed_copy(self.buffer.at[slot], slot).start()

            return slot

        def take_handed(self, i):
            slot = nearest(i) * 2 + 1 - core0
            self.handed_copy(self.src, slot).wait_recv()
            return slot

        def sent(self):
            def body(i, _):
                slot = nearest(i) * 2 + core0

                @pl.when(i > 0)
                def _():
                    self.direct_copy(self.src, slot, r).wait_send()

                self.handed_copy(self.src, slot).wait_send()
                return 0

            lax.fori_loop(0, Z, body, 0)

    def drain():
        for end in list(open_ends.values()):
            end()

    barrier = pltpu.get_barrier_semaphore()

    def greet_row(d, _):
        pl.semaphore_signal(barrier, inc=1, device_id=(along_row(d), c), device_id_type=MESH)
        return 0

    def greet_col(d, _):
        pl.semaphore_signal(barrier, inc=1, device_id=(r, along_col(d)), device_id_type=MESH)
        return 0

    lax.fori_loop(1, R, greet_row, 0)
    lax.fori_loop(1, C, greet_col, 0)
    search = search_ref[...]
    local_b = contract(search, search, ((1,), (1,)))
    src_pts[r] = points_ref[...]
    tgt_pts[c] = points_ref[...]
    pl.semaphore_wait(barrier, R + C - 2)

    TGT, SRC, SRC2, DEG, SCAL, SCAL2, OUT, B1, B2, B3, A1, A2, A3, X1, X2 = range(15)
    my_points = lambda peer: points_ref
    col_all(TGT, my_points, tgt_pts, "start")
    sources = Spread(SRC, SRC2, src_pts)
    sources.start(points_ref)

    rows = 96
    piece = LANES // R

    def stage_square(part, square):
        wide = jnp.concatenate([square, jnp.zeros((rows, LANES - rows), jnp.float32)], axis=1)
        for i in range(R):
            if (i + 1) * piece <= rows:
                part[i] = wide[i * piece : (i + 1) * piece]
            else:
                live = max(0, rows - i * piece)
                rest = jnp.zeros((piece - live, LANES), jnp.float32)
                part[i] = jnp.concatenate([wide[i * piece : i * piece + live], rest], axis=0) if live else rest

    def round1(phase, part, inbox):
        row_all(phase, lambda peer: part.at[peer], inbox, "start")
        inbox[r] = part[r]

    def round2(phase, part, inbox, piece_ref, inbox2):
        row_all(phase, lambda peer: part.at[peer], inbox, "recv")
        value = inbox[0]
        for i in range(1, R):
            value = value + inbox[i]
        piece_ref[0] = value
        col_all(phase + 1, lambda peer: piece_ref.at[0], inbox2, "start")
        inbox2[c] = value

    def round3(phase, piece_ref, inbox2, result):
        col_all(phase + 1, lambda peer: piece_ref.at[0], inbox2, "recv")
        value = inbox2[0]
        for i in range(1, C):
            value = value + inbox2[i]
        piece_ref[1] = value * (1.0 / total)
        row_all(phase + 2, lambda peer: piece_ref.at[1], result, "start")
        result[r] = value * (1.0 / total)

    def finish(phase, piece_ref, result):
        row_all(phase + 2, lambda peer: piece_ref.at[1], result, "recv")
        square = jnp.concatenate([result[i] for i in range(R)], axis=0)
        return square[:rows, :rows]

    def small_sum(phase, squares, part, inbox, piece_ref, inbox2):
        flat = jnp.concatenate([pack(square) for square in squares], axis=0)
        part[0] = flat
        row_all(phase, lambda peer: part.at[0], inbox, "start")
        inbox[r] = flat
        row_all(phase, lambda peer: part.at[0], inbox, "recv")
        value = inbox[0]
        for i in range(1, R):
            value = value + inbox[i]
        piece_ref[0] = value
        col_all(phase + 1, lambda peer: piece_ref.at[0], inbox2, "start")
        inbox2[c] = value
        col_all(phase + 1, lambda peer: piece_ref.at[0], inbox2, "recv")
        value = inbox2[0]
        for i in range(1, C):
            value = value + inbox2[i]
        value = value * (1.0 / total)
        return [unpack(value[8 * i : 8 * i + 8]) for i in range(len(squares))]

    stage_square(b_part, local_b)
    round1(B1, b_part, b_in)

    def lift_target(d, _):
        peer = along_col(d)

        @pl.when(d > 0)
        def _():
            col_copy(TGT, points_ref, tgt_pts.at[peer], peer, peer).wait_recv()

        tgt_lift[:, pl.ds(pl.multiple_of(peer * n, n), n)] = lifted(tgt_pts[peer], rate, False)
        return 0

    lax.fori_loop(0, C, lift_target, 0)
    del open_ends[TGT, "recv"]
    round2(B1, b_part, b_in, b_piece, b_in2)

    deg[...] = jnp.zeros_like(deg)
    def affinities(slot):
        exponent = lax.dot_general(
            lifted(src_pts[slot], rate, True), tgt_lift[...], (((0,), (0,)), ((), ())),
            preferred_element_type=jnp.float32,
        )
        affinity = jnp.exp2(exponent)
        deg[...] += jnp.sum(affinity.reshape(n // 8, 8, C * n), axis=0)
        tile[pl.ds(pl.multiple_of(slot * n, n), n), :] = affinity.astype(jnp.bfloat16)
        return 0

    lax.fori_loop(0, Z, lambda i, _: affinities(sources.take(i)), 0)
    lax.fori_loop(0, Z, lambda i, _: affinities(sources.take_handed(i)), 0)

    window = lambda peer: deg.at[:, pl.ds(pl.multiple_of(peer * n, n), n)]
    col_all(DEG, window, deg_in, "start")
    deg_in[c] = deg[:, pl.ds(pl.multiple_of(c * n, n), n)]
    round3(B1, b_piece, b_in2, b_res)
    col_all(DEG, window, deg_in, "recv")
    sums = deg_in[0]
    for i in range(1, C):
        sums = sums + deg_in[i]
    degrees = jnp.sum(sums, axis=0, keepdims=True)
    root = lax.rsqrt(degrees)
    root = root * (1.5 - 0.5 * degrees * root * root)
    scal[r] = (search_ref[...] * root).astype(jnp.bfloat16)
    blocks = Spread(SCAL, SCAL2, scal)
    blocks.start(scal.at[r])

    gram_b = finish(B1, b_piece, b_res)
    gram_b_ref[...] = gram_b
    factor = inverse_factor(gram_b[:NEV, :NEV])
    solved = contract(factor, contract(factor, search_ref[:NEV, :], ((1,), (0,))), ((0,), (0,)))

    def near_images(i, _):
        slot = blocks.take(i)
        value = jnp.dot(
            scal[slot], tile[pl.ds(pl.multiple_of(slot * n, n), n), :],
            preferred_element_type=jnp.float32,
        )

        @pl.when(i == 0)
        def _():
            image[...] = value

        @pl.when(i > 0)
        def _():
            image[...] += value

        return 0

    lax.fori_loop(0, Z, near_images, 0)

    def handed_block(i, _):
        blocks.take_handed(i)
        return 0

    lax.fori_loop(0, Z, handed_block, 0)
    pairs = C // 2
    pair0 = c // 2

    def images(j, _):
        pair = lax.rem(pair0 + 1 + j, pairs)
        at = pl.ds(pl.multiple_of(pair * (2 * n), 2 * n), 2 * n)
        value = image[:, at]
        for i in range(Z):
            slot = i * 2 + 1 - core0
            value = value + jnp.dot(
                scal[slot], tile[pl.ds(pl.multiple_of(slot * n, n), n), at],
                preferred_element_type=jnp.float32,
            )
        for half in range(2):
            peer = pair * 2 + half
            outp[peer] = value[:, half * n : (half + 1) * n]

            @pl.when(peer != c)
            def _():
                col_copy(OUT, outp.at[peer], out_in.at[c], peer, c).start()

        return 0

    lax.fori_loop(0, pairs, images, 0)
    for end in ("recv", "send"):
        open_ends[OUT, end] = functools.partial(
            col_all, OUT, lambda peer: outp.at[peer], out_in, end
        )
    out_in[c] = outp[c]
    col_all(OUT, lambda peer: outp.at[peer], out_in, "recv")
    sums = out_in[0]
    for i in range(1, C):
        sums = sums + out_in[i]
    applied = sums * root
    applied_ref[...] = applied

    local_a = contract(search_ref[...], applied, ((1,), (1,)))
    stage_square(a_part, local_a)
    round1(A1, a_part, a_in)
    leading, images_gram = small_sum(
        X1, [local_a[:NEV, :NEV], contract(applied[:NEV], applied[:NEV], ((1,), (1,)))],
        x_part, x_in, x_piece, x_in2,
    )
    round2(A1, a_part, a_in, a_piece, a_in2)
    projected = contract(factor, leading, ((1,), (0,)))
    residual = applied[:NEV] - contract(leading, solved, ((0,), (0,)))
    residual_gram = images_gram - contract(projected, projected, ((0,), (0,)))
    factor_r = inverse_factor(residual_gram)
    round3(A1, a_piece, a_in2, a_res)
    q_ref[...] = contract(factor_r, residual, ((1,), (0,)))
    gram_a_ref[...] = finish(A1, a_piece, a_res)
    drain()


def per_device(R, C, points, search):
    dim, n = points.shape
    rows = search.shape[0]
    f32 = jnp.float32
    piece = LANES // R
    square = lambda: [
        pltpu.VMEM((R, piece, LANES), f32),
        pltpu.VMEM((R, piece, LANES), f32),
        pltpu.VMEM((2, piece, LANES), f32),
        pltpu.VMEM((C, piece, LANES), f32),
        pltpu.VMEM((R, piece, LANES), f32),
    ]
    small = lambda: [
        pltpu.VMEM((1, 16, LANES), f32),
        pltpu.VMEM((R, 16, LANES), f32),
        pltpu.VMEM((1, 16, LANES), f32),
        pltpu.VMEM((C, 16, LANES), f32),
    ]
    vmem = pl.BlockSpec(memory_space=pltpu.VMEM)
    most = max(R, C)
    return pl.pallas_call(
        functools.partial(kernel, R, C, n),
        out_shape=(
            jax.ShapeDtypeStruct((rows, n), f32),
            jax.ShapeDtypeStruct((rows, rows), f32),
            jax.ShapeDtypeStruct((rows, rows), f32),
            jax.ShapeDtypeStruct((NEV, n), f32),
        ),
        in_specs=[vmem, vmem],
        out_specs=(vmem, vmem, vmem, vmem),
        scratch_shapes=[
            pltpu.VMEM((R, dim, n), f32),
            pltpu.VMEM((C, dim, n), f32),
            pltpu.VMEM((DEPTH, C * n), jnp.bfloat16),
            pltpu.VMEM((R * n, C * n), jnp.bfloat16),
            pltpu.VMEM((8, C * n), f32),
            pltpu.VMEM((C, 8, n), f32),
            pltpu.VMEM((R, rows, n), jnp.bfloat16),
            pltpu.VMEM((C, rows, n), f32),
            pltpu.VMEM((C, rows, n), f32),
            *square(),
            *square(),
            *small(),
            pltpu.VMEM((rows, C * n), f32),
            pltpu.SemaphoreType.DMA((15, most)),
            pltpu.SemaphoreType.DMA((15, most)),
        ],
        compiler_params=pltpu.CompilerParams(
            collective_id=0, has_side_effects=True, vmem_limit_bytes=60 << 20
        ),
    )(points, search)


def solution(mesh):
    placed = (P(None, ("row", "col")), P(None, ("row", "col")))
    return jax.shard_map(
        functools.partial(per_device, mesh.shape["row"], mesh.shape["col"]),
        mesh=mesh,
        in_specs=placed,
        out_specs=(P(None, ("row", "col")), P(), P(), P(None, ("row", "col"))),
        check_vma=False,
    )
```

```python
import functools
import math

import jax
import jax.numpy as jnp
from jax import lax
from jax.experimental import pallas as pl
from jax.experimental.pallas import tpu as pltpu
from jax.sharding import PartitionSpec as P

NEV = 32
MESH = pl.DeviceIdType.MESH
HIGH = lax.Precision.HIGHEST
DEPTH = 256
LANES = 128


TGT, SRC, SRC2, DEG, SCAL, SCAL2, O1, O2, O3, O4, B1, B2, B3, A1, A2, A3, X1, X2 = range(18)
PHASES = 18


def contract(a, b, dims):
    return lax.dot_general(
        a, b, (dims, ((), ())), precision=HIGH, preferred_element_type=jnp.float32
    )


def split3(x):
    hi = x.astype(jnp.bfloat16)
    rest = x - hi.astype(jnp.float32)
    mid = rest.astype(jnp.bfloat16)
    low = (rest - mid.astype(jnp.float32)).astype(jnp.bfloat16)
    return hi, mid, low


def lifted(x, rate, is_source):
    dim, n = x.shape
    squares = jnp.broadcast_to(-rate * jnp.sum(x * x, axis=0, keepdims=True), (16, n))
    row = lax.broadcasted_iota(jnp.int32, (16, n), 0)
    parts = split3(squares)
    one = jnp.ones((16, n), jnp.float32)
    first = jnp.where(row == 0, parts[0].astype(jnp.float32), 0.0)
    first = jnp.where(row == 1, parts[1].astype(jnp.float32), first)
    first = jnp.where(row == 2, parts[2].astype(jnp.float32), first)
    second = jnp.where(row < 3, one, 0.0)
    if is_source:
        hi, mid, low = split3(x)
        blocks = [hi, hi, mid, hi, low, mid]
        extra = [first, second]
    else:
        hi, mid, low = split3(x * (2.0 * rate))
        blocks = [hi, mid, hi, low, hi, mid]
        extra = [second, first]
    blocks = blocks + [e.astype(jnp.bfloat16) for e in extra]
    used = 6 * dim + 32
    if used < DEPTH:
        blocks.append(jnp.zeros((DEPTH - used, n), jnp.bfloat16))
    return jnp.concatenate(blocks, axis=0)


def inverse_factor(gram):
    k = gram.shape[0]
    row = lax.broadcasted_iota(jnp.int32, (k, k), 0)
    col = lax.broadcasted_iota(jnp.int32, (k, k), 1)
    eye = jnp.where(row == col, 1.0, 0.0)
    pad = jnp.zeros((k, LANES - 2 * k), jnp.float32)
    work = jnp.concatenate([gram, eye, pad], axis=1)
    below = lax.broadcasted_iota(jnp.int32, (k, 1), 0)
    for step in range(k):
        pivot_row = work[step : step + 1, :]
        pivot = work[step : step + 1, step : step + 1]
        factor = jnp.where(below > step, work[:, step : step + 1] / pivot, 0.0)
        work = work - factor * pivot_row
    diagonal = jnp.sum(work[:, :k] * eye, axis=1, keepdims=True)
    return work[:, k : 2 * k] * lax.rsqrt(diagonal)


def grid_x(C):
    size = 1
    while size * size < C:
        size *= 2
    return size


def pack(square):
    return jnp.concatenate([square[8 * i : 8 * i + 8, :] for i in range(4)], axis=1)


def unpack(flat):
    return jnp.concatenate([flat[:, 32 * i : 32 * i + 32] for i in range(4)], axis=0)


def kernel(
    R, C, n, points_ref, search_ref, applied_ref, gram_a_ref, gram_b_ref, q_ref,
    src_pts, tgt_pts, tgt_lift, tile, deg, deg_in, scal, outp,
    along_x, along_y, middle_x, middle_y, last_x, last_y,
    a_part, a_in, a_piece, a_in2, a_res,
    b_part, b_in, b_piece, b_in2, b_res,
    x_part, x_in, x_piece, x_in2, image,
    ssem, rsem,
):
    r = lax.axis_index("row")
    c = lax.axis_index("col")
    total = R * C * n
    SINGLY = {TGT: C, SRC: R // 2, SRC2: R // 2, SCAL: R // 2}
    rate = (2.0 / points_ref.shape[0]) * math.log2(math.e)

    def along_row(d):
        return lax.rem(r + d, R)

    def along_col(d):
        return lax.rem(c + d, C)

    def arrived(phase, slot):
        if phase not in SINGLY:
            return rsem.at[phase]
        first = PHASES + sum(SINGLY[p] for p in SINGLY if p < phase)
        return rsem.at[first + slot]

    def row_copy(phase, src, dst, peer, slot):
        return pltpu.make_async_remote_copy(
            src_ref=src, dst_ref=dst, send_sem=ssem.at[phase], recv_sem=arrived(phase, slot),
            device_id=(peer, c), device_id_type=MESH,
        )

    def col_copy(phase, src, dst, peer, slot):
        return pltpu.make_async_remote_copy(
            src_ref=src, dst_ref=dst, send_sem=ssem.at[phase], recv_sem=arrived(phase, slot),
            device_id=(r, peer), device_id_type=MESH,
        )

    open_ends = {}

    def await_blocks(copy, phase, buffer, count, what):
        blocks = buffer.at[pl.ds(0, count)]
        whole = copy(phase, blocks, blocks, 0, 0)
        if what == "recv":
            whole.wait_recv()
        else:
            whole.wait_send()

    def every(copy, me, size, phase, src_of, dst, what):
        def body(d, _):
            peer = lax.rem(me + d, size)
            copy(phase, src_of(peer), dst.at[me], peer, me).start()
            return 0

        if what == "start":
            for end in ("recv", "send"):
                open_ends[phase, end] = functools.partial(
                    every, copy, me, size, phase, src_of, dst, end
                )
            lax.fori_loop(1, size, body, 0)
        else:
            del open_ends[phase, what]
            await_blocks(copy, phase, dst, size - 1, what)

    row_all = functools.partial(every, row_copy, r, R)
    col_all = functools.partial(every, col_copy, c, C)

    Z = R // 2
    z0, core0 = r // 2, lax.rem(r, 2)
    partner = z0 * 2 + 1 - core0
    X = grid_x(C)
    Y = C // X
    y, x = c // X, lax.rem(c, X)
    split = search_ref.shape[0] // 2

    def nearest(i):
        half = (i + 1) // 2
        return lax.rem(z0 + jnp.where(lax.rem(i, 2) == 1, half, Z - half), Z)

    class Spread:
        def __init__(self, direct, handed, buffer):
            self.direct, self.handed, self.buffer = direct, handed, buffer

        def direct_copy(self, src, peer, slot):
            return pltpu.make_async_remote_copy(
                src_ref=src, dst_ref=self.buffer.at[slot], send_sem=ssem.at[self.direct],
                recv_sem=arrived(self.direct, slot // 2), device_id=(peer, c), device_id_type=MESH,
            )

        def handed_copy(self, src, slot):
            return pltpu.make_async_remote_copy(
                src_ref=src, dst_ref=self.buffer.at[slot], send_sem=ssem.at[self.handed],
                recv_sem=arrived(self.handed, slot // 2), device_id=(partner, c), device_id_type=MESH,
            )

        def start(self, src):
            self.src = src

            def body(i, _):
                self.direct_copy(src, nearest(i) * 2 + core0, r).start()
                return 0

            self.handed_copy(src, r).start()
            lax.fori_loop(1, Z, body, 0)
            open_ends[self.direct, "send"] = self.sent

        def take(self, i):
            slot = nearest(i) * 2 + core0

            @pl.when(i > 0)
            def _():
                self.direct_copy(self.src, slot, slot).wait_recv()
                self.handed_copy(self.buffer.at[slot], slot).start()

            return slot

        def take_handed(self, i):
            slot = nearest(i) * 2 + 1 - core0
            self.handed_copy(self.src, slot).wait_recv()
            return slot

        def take_all_handed(self):
            await_blocks(row_copy, self.handed, self.buffer, Z, "recv")

        def sent(self):
            await_blocks(row_copy, self.direct, self.buffer, Z - 1, "send")
            await_blocks(row_copy, self.handed, self.buffer, Z, "send")

    def drain():
        for end in list(open_ends.values()):
            end()

    barrier = pltpu.get_barrier_semaphore()

    def greet_row(d, _):
        pl.semaphore_signal(barrier, inc=1, device_id=(along_row(d), c), device_id_type=MESH)
        return 0

    def greet_col(d, _):
        pl.semaphore_signal(barrier, inc=1, device_id=(r, along_col(d)), device_id_type=MESH)
        return 0

    lax.fori_loop(1, R, greet_row, 0)
    lax.fori_loop(1, C, greet_col, 0)
    search = search_ref[...]
    local_b = contract(search, search, ((1,), (1,)))
    src_pts[r] = points_ref[...]
    tgt_pts[c] = points_ref[...]
    pl.semaphore_wait(barrier, R + C - 2)

    my_points = lambda peer: points_ref
    col_all(TGT, my_points, tgt_pts, "start")
    sources = Spread(SRC, SRC2, src_pts)
    sources.start(points_ref)

    rows = 96
    piece = LANES // R

    def stage_square(part, square):
        wide = jnp.concatenate([square, jnp.zeros((rows, LANES - rows), jnp.float32)], axis=1)
        for i in range(R):
            if (i + 1) * piece <= rows:
                part[i] = wide[i * piece : (i + 1) * piece]
            else:
                live = max(0, rows - i * piece)
                rest = jnp.zeros((piece - live, LANES), jnp.float32)
                part[i] = jnp.concatenate([wide[i * piece : i * piece + live], rest], axis=0) if live else rest

    def round1(phase, part, inbox):
        row_all(phase, lambda peer: part.at[peer], inbox, "start")
        inbox[r] = part[r]

    def round2(phase, part, inbox, piece_ref, inbox2):
        row_all(phase, lambda peer: part.at[peer], inbox, "recv")
        value = inbox[0]
        for i in range(1, R):
            value = value + inbox[i]
        piece_ref[0] = value
        col_all(phase + 1, lambda peer: piece_ref.at[0], inbox2, "start")
        inbox2[c] = value

    def round3(phase, piece_ref, inbox2, result):
        col_all(phase + 1, lambda peer: piece_ref.at[0], inbox2, "recv")
        value = inbox2[0]
        for i in range(1, C):
            value = value + inbox2[i]
        piece_ref[1] = value * (1.0 / total)
        row_all(phase + 2, lambda peer: piece_ref.at[1], result, "start")
        result[r] = value * (1.0 / total)

    def finish(phase, piece_ref, result):
        row_all(phase + 2, lambda peer: piece_ref.at[1], result, "recv")
        square = jnp.concatenate([result[i] for i in range(R)], axis=0)
        return square[:rows, :rows]

    def small_sum(phase, squares, part, inbox, piece_ref, inbox2):
        flat = jnp.concatenate([pack(square) for square in squares], axis=0)
        part[0] = flat
        row_all(phase, lambda peer: part.at[0], inbox, "start")
        inbox[r] = flat
        row_all(phase, lambda peer: part.at[0], inbox, "recv")
        value = inbox[0]
        for i in range(1, R):
            value = value + inbox[i]
        piece_ref[0] = value
        col_all(phase + 1, lambda peer: piece_ref.at[0], inbox2, "start")
        inbox2[c] = value
        col_all(phase + 1, lambda peer: piece_ref.at[0], inbox2, "recv")
        value = inbox2[0]
        for i in range(1, C):
            value = value + inbox2[i]
        value = value * (1.0 / total)
        return [unpack(value[8 * i : 8 * i + 8]) for i in range(len(squares))]

    stage_square(b_part, local_b)
    round1(B1, b_part, b_in)

    def lift_target(d, _):
        peer = along_col(d)

        @pl.when(d > 0)
        def _():
            col_copy(TGT, points_ref, tgt_pts.at[peer], peer, peer).wait_recv()

        tgt_lift[:, pl.ds(pl.multiple_of(peer * n, n), n)] = lifted(tgt_pts[peer], rate, False)
        return 0

    lax.fori_loop(0, C, lift_target, 0)
    del open_ends[TGT, "recv"]
    round2(B1, b_part, b_in, b_piece, b_in2)

    deg[...] = jnp.zeros_like(deg)
    def affinities(slot):
        exponent = lax.dot_general(
            lifted(src_pts[slot], rate, True), tgt_lift[...], (((0,), (0,)), ((), ())),
            preferred_element_type=jnp.float32,
        )
        affinity = jnp.exp2(exponent)
        deg[...] += jnp.sum(affinity.reshape(n // 8, 8, C * n), axis=0)
        tile[pl.ds(pl.multiple_of(slot * n, n), n), :] = affinity.astype(jnp.bfloat16)
        return 0

    lax.fori_loop(0, Z, lambda i, _: affinities(sources.take(i)), 0)
    lax.fori_loop(0, Z, lambda i, _: affinities(sources.take_handed(i)), 0)

    window = lambda peer: deg.at[:, pl.ds(pl.multiple_of(peer * n, n), n)]
    col_all(DEG, window, deg_in, "start")
    deg_in[c] = deg[:, pl.ds(pl.multiple_of(c * n, n), n)]
    round3(B1, b_piece, b_in2, b_res)
    col_all(DEG, window, deg_in, "recv")
    sums = deg_in[0]
    for i in range(1, C):
        sums = sums + deg_in[i]
    degrees = jnp.sum(sums, axis=0, keepdims=True)
    root = lax.rsqrt(degrees)
    root = root * (1.5 - 0.5 * degrees * root * root)
    scal[r] = (search_ref[...] * root).astype(jnp.bfloat16)
    blocks = Spread(SCAL, SCAL2, scal)
    blocks.start(scal.at[r])

    gram_b = finish(B1, b_piece, b_res)
    gram_b_ref[...] = gram_b
    factor = inverse_factor(gram_b[:NEV, :NEV])
    solved = contract(factor, contract(factor, search_ref[:NEV, :], ((1,), (0,))), ((0,), (0,)))

    def near_images(i, _):
        slot = blocks.take(i)
        value = jnp.dot(
            scal[slot], tile[pl.ds(pl.multiple_of(slot * n, n), n), :],
            preferred_element_type=jnp.float32,
        )

        @pl.when(i == 0)
        def _():
            image[...] = value

        @pl.when(i > 0)
        def _():
            image[...] += value

        return 0

    lax.fori_loop(0, Z, near_images, 0)

    blocks.take_all_handed()
    pairs = C // 2
    pair0 = c // 2

    def images(j, _):
        pair = lax.rem(pair0 + 1 + j, pairs)
        at = pl.ds(pl.multiple_of(pair * (2 * n), 2 * n), 2 * n)
        value = image[:, at]
        for i in range(Z):
            slot = i * 2 + 1 - core0
            value = value + jnp.dot(
                scal[slot], tile[pl.ds(pl.multiple_of(slot * n, n), n), at],
                preferred_element_type=jnp.float32,
            )
        for half in range(2):
            block = pair * 2 + half
            by, bx = block // X, lax.rem(block, X)
            mine = value[:, half * n : (half + 1) * n]
            outp[block, 0] = mine[:split]
            outp[block, 1] = mine[split:]

            @pl.when(bx != x)
            def _():
                col_copy(O1, outp.at[block, 0], along_x.at[x * Y + by], y * X + bx, 0).start()

            @pl.when(bx == x)
            def _():
                along_x[x * Y + by] = mine[:split]

            @pl.when(by != y)
            def _():
                col_copy(O2, outp.at[block, 1], along_y.at[y * X + bx], by * X + x, 0).start()

            @pl.when(by == y)
            def _():
                along_y[y * X + bx] = mine[split:]

        return 0

    lax.fori_loop(0, pairs, images, 0)

    def second(phase, inbox, count, size, me, device, middle, last, phase_out):
        if count > 1:
            await_blocks(col_copy, phase, inbox, (count - 1) * size, "recv")

        def body(i, _):
            at = lax.rem(me + 1 + i, size)
            value = inbox[at]
            for k in range(1, count):
                value = value + inbox[k * size + at]

            @pl.when(at != me)
            def _():
                middle[at] = value
                col_copy(phase_out, middle.at[at], last.at[me], device(at), 0).start()

            @pl.when(at == me)
            def _():
                last[me] = value

            return 0

        lax.fori_loop(0, size, body, 0)

    second(O1, along_x, X, Y, y, lambda at: at * X + x, middle_y, last_y, O3)
    second(O2, along_y, Y, X, x, lambda at: y * X + at, middle_x, last_x, O4)

    def ends(what):
        for phase, buffer, count in (
            (O1, along_x, (X - 1) * Y), (O2, along_y, (Y - 1) * X), (O3, last_y, Y - 1), (O4, last_x, X - 1),
        ):
            if count and not (what == "recv" and phase in (O1, O2)):
                await_blocks(col_copy, phase, buffer, count, what)

    ends("recv")
    open_ends[O1, "send"] = functools.partial(ends, "send")
    upper, lower = last_y[0], last_x[0]
    for i in range(1, Y):
        upper = upper + last_y[i]
    for i in range(1, X):
        lower = lower + last_x[i]
    sums = jnp.concatenate([upper, lower], axis=0)
    applied = sums * root
    applied_ref[...] = applied

    local_a = contract(search_ref[...], applied, ((1,), (1,)))
    stage_square(a_part, local_a)
    round1(A1, a_part, a_in)
    leading, images_gram = small_sum(
        X1, [local_a[:NEV, :NEV], contract(applied[:NEV], applied[:NEV], ((1,), (1,)))],
        x_part, x_in, x_piece, x_in2,
    )
    round2(A1, a_part, a_in, a_piece, a_in2)
    projected = contract(factor, leading, ((1,), (0,)))
    residual = applied[:NEV] - contract(leading, solved, ((0,), (0,)))
    residual_gram = images_gram - contract(projected, projected, ((0,), (0,)))
    factor_r = inverse_factor(residual_gram)
    round3(A1, a_piece, a_in2, a_res)
    q_ref[...] = contract(factor_r, residual, ((1,), (0,)))
    gram_a_ref[...] = finish(A1, a_piece, a_res)
    drain()


def per_device(R, C, points, search):
    dim, n = points.shape
    rows = search.shape[0]
    f32 = jnp.float32
    piece = LANES // R
    square = lambda: [
        pltpu.VMEM((R, piece, LANES), f32),
        pltpu.VMEM((R, piece, LANES), f32),
        pltpu.VMEM((2, piece, LANES), f32),
        pltpu.VMEM((C, piece, LANES), f32),
        pltpu.VMEM((R, piece, LANES), f32),
    ]
    small = lambda: [
        pltpu.VMEM((1, 16, LANES), f32),
        pltpu.VMEM((R, 16, LANES), f32),
        pltpu.VMEM((1, 16, LANES), f32),
        pltpu.VMEM((C, 16, LANES), f32),
    ]
    vmem = pl.BlockSpec(memory_space=pltpu.VMEM)
    X = grid_x(C)
    singly = C + 3 * (R // 2)
    return pl.pallas_call(
        functools.partial(kernel, R, C, n),
        out_shape=(
            jax.ShapeDtypeStruct((rows, n), f32),
            jax.ShapeDtypeStruct((rows, rows), f32),
            jax.ShapeDtypeStruct((rows, rows), f32),
            jax.ShapeDtypeStruct((NEV, n), f32),
        ),
        in_specs=[vmem, vmem],
        out_specs=(vmem, vmem, vmem, vmem),
        scratch_shapes=[
            pltpu.VMEM((R, dim, n), f32),
            pltpu.VMEM((C, dim, n), f32),
            pltpu.VMEM((DEPTH, C * n), jnp.bfloat16),
            pltpu.VMEM((R * n, C * n), jnp.bfloat16),
            pltpu.VMEM((8, C * n), f32),
            pltpu.VMEM((C, 8, n), f32),
            pltpu.VMEM((R, rows, n), jnp.bfloat16),
            pltpu.VMEM((C, 2, rows // 2, n), f32),
            pltpu.VMEM((C, rows // 2, n), f32),
            pltpu.VMEM((C, rows // 2, n), f32),
            pltpu.VMEM((X, rows // 2, n), f32),
            pltpu.VMEM((C // X, rows // 2, n), f32),
            pltpu.VMEM((X, rows // 2, n), f32),
            pltpu.VMEM((C // X, rows // 2, n), f32),
            *square(),
            *square(),
            *small(),
            pltpu.VMEM((rows, C * n), f32),
            pltpu.SemaphoreType.DMA((PHASES,)),
            pltpu.SemaphoreType.DMA((PHASES + singly,)),
        ],
        compiler_params=pltpu.CompilerParams(
            collective_id=0, has_side_effects=True, vmem_limit_bytes=60 << 20
        ),
    )(points, search)


def solution(mesh):
    placed = (P(None, ("row", "col")), P(None, ("row", "col")))
    return jax.shard_map(
        functools.partial(per_device, mesh.shape["row"], mesh.shape["col"]),
        mesh=mesh,
        in_specs=placed,
        out_specs=(P(None, ("row", "col")), P(), P(), P(None, ("row", "col"))),
        check_vma=False,
    )
```

```python
import functools
import math

import jax
import jax.numpy as jnp
from jax import lax
from jax.experimental import pallas as pl
from jax.experimental.pallas import tpu as pltpu
from jax.sharding import PartitionSpec as P

NEV = 32
MESH = pl.DeviceIdType.MESH
HIGH = lax.Precision.HIGHEST
DEPTH = 256
LANES = 128


TGT, SRC, SRC2, DEG, SCAL, SCAL2, O1, O2, O3, O4, B1, B2, B3, A1, A2, A3, X1, X2 = range(18)
PHASES = 18
NEAR = 3


def contract(a, b, dims):
    return lax.dot_general(
        a, b, (dims, ((), ())), precision=HIGH, preferred_element_type=jnp.float32
    )


def split3(x):
    hi = x.astype(jnp.bfloat16)
    rest = x - hi.astype(jnp.float32)
    mid = rest.astype(jnp.bfloat16)
    low = (rest - mid.astype(jnp.float32)).astype(jnp.bfloat16)
    return hi, mid, low


def lifted(x, rate, is_source):
    dim, n = x.shape
    squares = jnp.broadcast_to(-rate * jnp.sum(x * x, axis=0, keepdims=True), (16, n))
    row = lax.broadcasted_iota(jnp.int32, (16, n), 0)
    parts = split3(squares)
    one = jnp.ones((16, n), jnp.float32)
    first = jnp.where(row == 0, parts[0].astype(jnp.float32), 0.0)
    first = jnp.where(row == 1, parts[1].astype(jnp.float32), first)
    first = jnp.where(row == 2, parts[2].astype(jnp.float32), first)
    second = jnp.where(row < 3, one, 0.0)
    if is_source:
        hi, mid, low = split3(x)
        blocks = [hi, hi, mid, hi, low, mid]
        extra = [first, second]
    else:
        hi, mid, low = split3(x * (2.0 * rate))
        blocks = [hi, mid, hi, low, hi, mid]
        extra = [second, first]
    blocks = blocks + [e.astype(jnp.bfloat16) for e in extra]
    used = 6 * dim + 32
    if used < DEPTH:
        blocks.append(jnp.zeros((DEPTH - used, n), jnp.bfloat16))
    return jnp.concatenate(blocks, axis=0)


def inverse_factor(gram):
    k = gram.shape[0]
    row = lax.broadcasted_iota(jnp.int32, (k, k), 0)
    col = lax.broadcasted_iota(jnp.int32, (k, k), 1)
    eye = jnp.where(row == col, 1.0, 0.0)
    pad = jnp.zeros((k, LANES - 2 * k), jnp.float32)
    work = jnp.concatenate([gram, eye, pad], axis=1)
    below = lax.broadcasted_iota(jnp.int32, (k, 1), 0)
    for step in range(k):
        pivot_row = work[step : step + 1, :]
        pivot = work[step : step + 1, step : step + 1]
        factor = jnp.where(below > step, work[:, step : step + 1] / pivot, 0.0)
        work = work - factor * pivot_row
    diagonal = jnp.sum(work[:, :k] * eye, axis=1, keepdims=True)
    return work[:, k : 2 * k] * lax.rsqrt(diagonal)


def grid_x(C):
    size = 1
    while size * size < C:
        size *= 2
    return size


def nearest_first(X, Y):
    hops = lambda d, size: min(d, size - d)
    steps = [(hops(dy, Y) + hops(dx, X), dy * X + dx) for dy in range(Y) for dx in range(X)]
    return [step for _, step in sorted(steps)]


def chosen(i, values):
    result = values[0]
    for k, value in enumerate(values):
        result = jnp.where(i == k, value, result)
    return result


def pack(square):
    return jnp.concatenate([square[8 * i : 8 * i + 8, :] for i in range(4)], axis=1)


def unpack(flat):
    return jnp.concatenate([flat[:, 32 * i : 32 * i + 32] for i in range(4)], axis=0)


def kernel(
    R, C, n, points_ref, search_ref, applied_ref, gram_a_ref, gram_b_ref, q_ref,
    src_pts, tgt_pts, tgt_lift, tile, deg, deg_in, scal, outp,
    along_x, along_y, middle_x, middle_y, last_x, last_y,
    a_part, a_in, a_piece, a_in2, a_res,
    b_part, b_in, b_piece, b_in2, b_res,
    x_part, x_in, x_piece, x_in2, image, src_lift,
    ssem, rsem,
):
    r = lax.axis_index("row")
    c = lax.axis_index("col")
    total = R * C * n
    SINGLY = {TGT: C, SRC: R // 2, SRC2: R // 2, SCAL: R // 2}
    rate = (2.0 / points_ref.shape[0]) * math.log2(math.e)

    def along_row(d):
        return lax.rem(r + d, R)

    def along_col(d):
        return lax.rem(c + d, C)

    def arrived(phase, slot):
        if phase not in SINGLY:
            return rsem.at[phase]
        first = PHASES + sum(SINGLY[p] for p in SINGLY if p < phase)
        return rsem.at[first + slot]

    def row_copy(phase, src, dst, peer, slot):
        return pltpu.make_async_remote_copy(
            src_ref=src, dst_ref=dst, send_sem=ssem.at[phase], recv_sem=arrived(phase, slot),
            device_id=(peer, c), device_id_type=MESH,
        )

    def col_copy(phase, src, dst, peer, slot):
        return pltpu.make_async_remote_copy(
            src_ref=src, dst_ref=dst, send_sem=ssem.at[phase], recv_sem=arrived(phase, slot),
            device_id=(r, peer), device_id_type=MESH,
        )

    open_ends = {}

    def await_blocks(copy, phase, buffer, count, what):
        blocks = buffer.at[pl.ds(0, count)]
        whole = copy(phase, blocks, blocks, 0, 0)
        if what == "recv":
            whole.wait_recv()
        else:
            whole.wait_send()

    def every(copy, me, size, phase, src_of, dst, what):
        def body(d, _):
            peer = lax.rem(me + d, size)
            copy(phase, src_of(peer), dst.at[me], peer, me).start()
            return 0

        if what == "start":
            for end in ("recv", "send"):
                open_ends[phase, end] = functools.partial(
                    every, copy, me, size, phase, src_of, dst, end
                )
            lax.fori_loop(1, size, body, 0)
        else:
            del open_ends[phase, what]
            await_blocks(copy, phase, dst, size - 1, what)

    row_all = functools.partial(every, row_copy, r, R)
    col_all = functools.partial(every, col_copy, c, C)

    Z = R // 2
    z0, core0 = r // 2, lax.rem(r, 2)
    partner = z0 * 2 + 1 - core0
    X = grid_x(C)
    Y = C // X
    y, x = c // X, lax.rem(c, X)
    split = search_ref.shape[0] // 2
    near = min(NEAR, Z)

    def nearest(i):
        half = (i + 1) // 2
        return lax.rem(z0 + jnp.where(lax.rem(i, 2) == 1, half, Z - half), Z)

    class Spread:
        def __init__(self, direct, handed, buffer):
            self.direct, self.handed, self.buffer = direct, handed, buffer

        def direct_copy(self, src, peer, slot):
            return pltpu.make_async_remote_copy(
                src_ref=src, dst_ref=self.buffer.at[slot], send_sem=ssem.at[self.direct],
                recv_sem=arrived(self.direct, slot // 2), device_id=(peer, c), device_id_type=MESH,
            )

        def handed_copy(self, src, slot):
            return pltpu.make_async_remote_copy(
                src_ref=src, dst_ref=self.buffer.at[slot], send_sem=ssem.at[self.handed],
                recv_sem=arrived(self.handed, slot // 2), device_id=(partner, c), device_id_type=MESH,
            )

        def start(self, src):
            self.src = src

            def body(i, _):
                self.direct_copy(src, nearest(i) * 2 + core0, r).start()
                return 0

            self.handed_copy(src, r).start()
            lax.fori_loop(1, Z, body, 0)
            open_ends[self.direct, "send"] = self.sent

        def take(self, i):
            slot = nearest(i) * 2 + core0

            def step():
                self.direct_copy(self.src, slot, slot).wait_recv()
                self.handed_copy(self.buffer.at[slot], slot).start()

            step() if isinstance(i, int) else pl.when(i > 0)(step)

            return slot

        def take_handed(self, i):
            slot = nearest(i) * 2 + 1 - core0
            self.handed_copy(self.src, slot).wait_recv()
            return slot

        def take_all_handed(self):
            await_blocks(row_copy, self.handed, self.buffer, Z, "recv")

        def sent(self):
            await_blocks(row_copy, self.direct, self.buffer, Z - 1, "send")
            await_blocks(row_copy, self.handed, self.buffer, Z, "send")

    def drain():
        for end in list(open_ends.values()):
            end()

    barrier = pltpu.get_barrier_semaphore()

    def greet_row(d, _):
        pl.semaphore_signal(barrier, inc=1, device_id=(along_row(d), c), device_id_type=MESH)
        return 0

    def greet_col(d, _):
        pl.semaphore_signal(barrier, inc=1, device_id=(r, along_col(d)), device_id_type=MESH)
        return 0

    lax.fori_loop(1, R, greet_row, 0)
    lax.fori_loop(1, C, greet_col, 0)
    search = search_ref[...]
    local_b = contract(search, search, ((1,), (1,)))
    src_pts[r] = points_ref[...]
    tgt_pts[c] = points_ref[...]
    pl.semaphore_wait(barrier, R + C - 2)

    my_points = lambda peer: points_ref
    col_all(TGT, my_points, tgt_pts, "start")
    sources = Spread(SRC, SRC2, src_pts)
    sources.start(points_ref)

    rows = 96
    piece = LANES // R

    def stage_square(part, square):
        wide = jnp.concatenate([square, jnp.zeros((rows, LANES - rows), jnp.float32)], axis=1)
        for i in range(R):
            if (i + 1) * piece <= rows:
                part[i] = wide[i * piece : (i + 1) * piece]
            else:
                live = max(0, rows - i * piece)
                rest = jnp.zeros((piece - live, LANES), jnp.float32)
                part[i] = jnp.concatenate([wide[i * piece : i * piece + live], rest], axis=0) if live else rest

    def round1(phase, part, inbox):
        row_all(phase, lambda peer: part.at[peer], inbox, "start")
        inbox[r] = part[r]

    def round2(phase, part, inbox, piece_ref, inbox2):
        row_all(phase, lambda peer: part.at[peer], inbox, "recv")
        value = inbox[0]
        for i in range(1, R):
            value = value + inbox[i]
        piece_ref[0] = value
        col_all(phase + 1, lambda peer: piece_ref.at[0], inbox2, "start")
        inbox2[c] = value

    def round3(phase, piece_ref, inbox2, result):
        col_all(phase + 1, lambda peer: piece_ref.at[0], inbox2, "recv")
        value = inbox2[0]
        for i in range(1, C):
            value = value + inbox2[i]
        piece_ref[1] = value * (1.0 / total)
        row_all(phase + 2, lambda peer: piece_ref.at[1], result, "start")
        result[r] = value * (1.0 / total)

    def finish(phase, piece_ref, result):
        row_all(phase + 2, lambda peer: piece_ref.at[1], result, "recv")
        square = jnp.concatenate([result[i] for i in range(R)], axis=0)
        return square[:rows, :rows]

    def small_start(phase, squares, part, inbox):
        flat = jnp.concatenate([pack(square) for square in squares], axis=0)
        part[0] = flat
        inbox[r] = flat
        row_all(phase, lambda peer: part.at[0], inbox, "start")

    def small_turn(phase, part, inbox, piece_ref, inbox2):
        row_all(phase, lambda peer: part.at[0], inbox, "recv")
        value = inbox[0]
        for i in range(1, R):
            value = value + inbox[i]
        piece_ref[0] = value
        inbox2[c] = value
        col_all(phase + 1, lambda peer: piece_ref.at[0], inbox2, "start")

    def small_finish(phase, piece_ref, inbox2, count):
        col_all(phase + 1, lambda peer: piece_ref.at[0], inbox2, "recv")
        value = inbox2[0]
        for i in range(1, C):
            value = value + inbox2[i]
        value = value * (1.0 / total)
        return [unpack(value[8 * i : 8 * i + 8]) for i in range(count)]

    stage_square(b_part, local_b)
    round1(B1, b_part, b_in)

    def affinities(exponent, slots, at, width):
        affinity = jnp.exp2(exponent)
        rows_in = n * len(slots)
        deg[:, at] += jnp.sum(affinity.reshape(rows_in // 8, 8, width), axis=0)
        low = affinity.astype(jnp.bfloat16)
        for i, slot in enumerate(slots):
            tile[pl.ds(pl.multiple_of(slot * n, n), n), at] = low[i * n : (i + 1) * n]

    def cross(lifted_sources, lifted_targets):
        return lax.dot_general(
            lifted_sources, lifted_targets, (((0,), (0,)), ((), ())),
            preferred_element_type=jnp.float32,
        )

    deg[...] = jnp.zeros_like(deg)
    early = [r, partner]
    src_lift[:, 0:n] = lifted(points_ref[...], rate, True)
    sources.take_handed(0)
    src_lift[:, n : 2 * n] = lifted(src_pts[partner], rate, True)
    for i in range(1, near):
        early.append(sources.take(i))
        src_lift[:, (i + 1) * n : (i + 2) * n] = lifted(src_pts[early[-1]], rate, True)

    def early_cells(i, _):
        away = chosen(i, nearest_first(X, Y))
        peer = lax.rem(y + away // X, Y) * X + lax.rem(x + lax.rem(away, X), X)

        @pl.when(i > 0)
        def _():
            col_copy(TGT, points_ref, tgt_pts.at[peer], peer, peer).wait_recv()

        at = pl.ds(pl.multiple_of(peer * n, n), n)
        targets = lifted(tgt_pts[peer], rate, False)
        tgt_lift[:, at] = targets
        affinities(cross(src_lift[...], targets), early, at, n)
        return 0

    lax.fori_loop(0, C, early_cells, 0)
    del open_ends[TGT, "recv"]
    round2(B1, b_part, b_in, b_piece, b_in2)

    def block_row(slot):
        affinities(
            cross(lifted(src_pts[slot], rate, True), tgt_lift[...]), [slot], slice(None), C * n
        )
        return 0

    lax.fori_loop(near, Z, lambda i, _: block_row(sources.take(i)), 0)
    lax.fori_loop(1, Z, lambda i, _: block_row(sources.take_handed(i)), 0)

    window = lambda peer: deg.at[:, pl.ds(pl.multiple_of(peer * n, n), n)]
    col_all(DEG, window, deg_in, "start")
    deg_in[c] = deg[:, pl.ds(pl.multiple_of(c * n, n), n)]
    round3(B1, b_piece, b_in2, b_res)
    col_all(DEG, window, deg_in, "recv")
    sums = deg_in[0]
    for i in range(1, C):
        sums = sums + deg_in[i]
    degrees = jnp.sum(sums, axis=0, keepdims=True)
    root = lax.rsqrt(degrees)
    root = root * (1.5 - 0.5 * degrees * root * root)
    scal[r] = (search_ref[...] * root).astype(jnp.bfloat16)
    blocks = Spread(SCAL, SCAL2, scal)
    blocks.start(scal.at[r])

    gram_b = finish(B1, b_piece, b_res)
    gram_b_ref[...] = gram_b
    factor = inverse_factor(gram_b[:NEV, :NEV])
    solved = contract(factor, contract(factor, search_ref[:NEV, :], ((1,), (0,))), ((0,), (0,)))

    def near_images(i, _):
        slot = blocks.take(i)
        value = jnp.dot(
            scal[slot], tile[pl.ds(pl.multiple_of(slot * n, n), n), :],
            preferred_element_type=jnp.float32,
        )

        @pl.when(i == 0)
        def _():
            image[...] = value

        @pl.when(i > 0)
        def _():
            image[...] += value

        return 0

    lax.fori_loop(0, Z, near_images, 0)

    blocks.take_all_handed()
    pairs = C // 2
    pair0 = c // 2

    def images(j, _):
        pair = lax.rem(pair0 + 1 + j, pairs)
        at = pl.ds(pl.multiple_of(pair * (2 * n), 2 * n), 2 * n)
        value = image[:, at]
        for i in range(Z):
            slot = i * 2 + 1 - core0
            value = value + jnp.dot(
                scal[slot], tile[pl.ds(pl.multiple_of(slot * n, n), n), at],
                preferred_element_type=jnp.float32,
            )
        for half in range(2):
            block = pair * 2 + half
            by, bx = block // X, lax.rem(block, X)
            mine = value[:, half * n : (half + 1) * n]
            outp[block, 0] = mine[:split]
            outp[block, 1] = mine[split:]

            @pl.when(bx != x)
            def _():
                col_copy(O1, outp.at[block, 0], along_x.at[x * Y + by], y * X + bx, 0).start()

            @pl.when(bx == x)
            def _():
                along_x[x * Y + by] = mine[:split]

            @pl.when(by != y)
            def _():
                col_copy(O2, outp.at[block, 1], along_y.at[y * X + bx], by * X + x, 0).start()

            @pl.when(by == y)
            def _():
                along_y[y * X + bx] = mine[split:]

        return 0

    lax.fori_loop(0, pairs, images, 0)

    def second(phase, inbox, count, size, me, device, middle, last, phase_out):
        if count > 1:
            await_blocks(col_copy, phase, inbox, (count - 1) * size, "recv")

        def body(i, _):
            at = lax.rem(me + 1 + i, size)
            value = inbox[at]
            for k in range(1, count):
                value = value + inbox[k * size + at]

            @pl.when(at != me)
            def _():
                middle[at] = value
                col_copy(phase_out, middle.at[at], last.at[me], device(at), 0).start()

            @pl.when(at == me)
            def _():
                last[me] = value

            return 0

        lax.fori_loop(0, size, body, 0)

    second(O1, along_x, X, Y, y, lambda at: at * X + x, middle_y, last_y, O3)
    second(O2, along_y, Y, X, x, lambda at: y * X + at, middle_x, last_x, O4)

    def ends(what):
        for phase, buffer, count in (
            (O1, along_x, (X - 1) * Y), (O2, along_y, (Y - 1) * X), (O3, last_y, Y - 1), (O4, last_x, X - 1),
        ):
            if count and not (what == "recv" and phase in (O1, O2)):
                await_blocks(col_copy, phase, buffer, count, what)

    ends("recv")
    open_ends[O1, "send"] = functools.partial(ends, "send")
    upper, lower = last_y[0], last_x[0]
    for i in range(1, Y):
        upper = upper + last_y[i]
    for i in range(1, X):
        lower = lower + last_x[i]
    sums = jnp.concatenate([upper, lower], axis=0)
    applied = sums * root
    applied_ref[...] = applied

    leaders = jnp.concatenate([search_ref[:NEV, :], applied[:NEV]], axis=0)
    products = contract(leaders, applied[:NEV], ((1,), (1,)))
    small_start(X1, [products[:NEV], products[NEV:]], x_part, x_in)
    stage_square(a_part, contract(search_ref[...], applied, ((1,), (1,))))
    round1(A1, a_part, a_in)
    small_turn(X1, x_part, x_in, x_piece, x_in2)
    round2(A1, a_part, a_in, a_piece, a_in2)
    leading, images_gram = small_finish(X1, x_piece, x_in2, 2)
    projected = contract(factor, leading, ((1,), (0,)))
    residual_gram = images_gram - contract(projected, projected, ((0,), (0,)))
    round3(A1, a_piece, a_in2, a_res)
    residual = applied[:NEV] - contract(leading, solved, ((0,), (0,)))
    q_ref[...] = contract(inverse_factor(residual_gram), residual, ((1,), (0,)))
    gram_a_ref[...] = finish(A1, a_piece, a_res)
    drain()


def per_device(R, C, points, search):
    dim, n = points.shape
    rows = search.shape[0]
    f32 = jnp.float32
    piece = LANES // R
    square = lambda: [
        pltpu.VMEM((R, piece, LANES), f32),
        pltpu.VMEM((R, piece, LANES), f32),
        pltpu.VMEM((2, piece, LANES), f32),
        pltpu.VMEM((C, piece, LANES), f32),
        pltpu.VMEM((R, piece, LANES), f32),
    ]
    small = lambda: [
        pltpu.VMEM((1, 16, LANES), f32),
        pltpu.VMEM((R, 16, LANES), f32),
        pltpu.VMEM((1, 16, LANES), f32),
        pltpu.VMEM((C, 16, LANES), f32),
    ]
    vmem = pl.BlockSpec(memory_space=pltpu.VMEM)
    X = grid_x(C)
    singly = C + 3 * (R // 2)
    return pl.pallas_call(
        functools.partial(kernel, R, C, n),
        out_shape=(
            jax.ShapeDtypeStruct((rows, n), f32),
            jax.ShapeDtypeStruct((rows, rows), f32),
            jax.ShapeDtypeStruct((rows, rows), f32),
            jax.ShapeDtypeStruct((NEV, n), f32),
        ),
        in_specs=[vmem, vmem],
        out_specs=(vmem, vmem, vmem, vmem),
        scratch_shapes=[
            pltpu.VMEM((R, dim, n), f32),
            pltpu.VMEM((C, dim, n), f32),
            pltpu.VMEM((DEPTH, C * n), jnp.bfloat16),
            pltpu.VMEM((R * n, C * n), jnp.bfloat16),
            pltpu.VMEM((8, C * n), f32),
            pltpu.VMEM((C, 8, n), f32),
            pltpu.VMEM((R, rows, n), jnp.bfloat16),
            pltpu.VMEM((C, 2, rows // 2, n), f32),
            pltpu.VMEM((C, rows // 2, n), f32),
            pltpu.VMEM((C, rows // 2, n), f32),
            pltpu.VMEM((X, rows // 2, n), f32),
            pltpu.VMEM((C // X, rows // 2, n), f32),
            pltpu.VMEM((X, rows // 2, n), f32),
            pltpu.VMEM((C // X, rows // 2, n), f32),
            *square(),
            *square(),
            *small(),
            pltpu.VMEM((rows, C * n), f32),
            pltpu.VMEM((DEPTH, (min(NEAR, R // 2) + 1) * n), jnp.bfloat16),
            pltpu.SemaphoreType.DMA((PHASES,)),
            pltpu.SemaphoreType.DMA((PHASES + singly,)),
        ],
        compiler_params=pltpu.CompilerParams(
            collective_id=0, has_side_effects=True, vmem_limit_bytes=60 << 20
        ),
    )(points, search)


def solution(mesh):
    placed = (P(None, ("row", "col")), P(None, ("row", "col")))
    return jax.shard_map(
        functools.partial(per_device, mesh.shape["row"], mesh.shape["col"]),
        mesh=mesh,
        in_specs=placed,
        out_specs=(P(None, ("row", "col")), P(), P(), P(None, ("row", "col"))),
        check_vma=False,
    )
```

```python
import functools
import math

import jax
import jax.numpy as jnp
from jax import lax
from jax.experimental import pallas as pl
from jax.experimental.pallas import tpu as pltpu
from jax.sharding import PartitionSpec as P

NEV = 32
MESH = pl.DeviceIdType.MESH
HIGH = lax.Precision.HIGHEST
DEPTH = 256
LANES = 128


TGT, SRC, SRC2, DEG, SCAL, SCAL2, O1, O2, O3, O4, B1, B2, B3, A1, A2, A3, X1, X2 = range(18)
PHASES = 18
NEAR = 3


def contract(a, b, dims):
    return lax.dot_general(
        a, b, (dims, ((), ())), precision=HIGH, preferred_element_type=jnp.float32
    )


def split3(x):
    hi = x.astype(jnp.bfloat16)
    rest = x - hi.astype(jnp.float32)
    mid = rest.astype(jnp.bfloat16)
    low = (rest - mid.astype(jnp.float32)).astype(jnp.bfloat16)
    return hi, mid, low


def lifted(x, rate, is_source):
    dim, n = x.shape
    squares = jnp.broadcast_to(-rate * jnp.sum(x * x, axis=0, keepdims=True), (16, n))
    row = lax.broadcasted_iota(jnp.int32, (16, n), 0)
    parts = split3(squares)
    one = jnp.ones((16, n), jnp.float32)
    first = jnp.where(row == 0, parts[0].astype(jnp.float32), 0.0)
    first = jnp.where(row == 1, parts[1].astype(jnp.float32), first)
    first = jnp.where(row == 2, parts[2].astype(jnp.float32), first)
    second = jnp.where(row < 3, one, 0.0)
    if is_source:
        hi, mid, low = split3(x)
        blocks = [hi, hi, mid, hi, low, mid]
        extra = [first, second]
    else:
        hi, mid, low = split3(x * (2.0 * rate))
        blocks = [hi, mid, hi, low, hi, mid]
        extra = [second, first]
    blocks = blocks + [e.astype(jnp.bfloat16) for e in extra]
    used = 6 * dim + 32
    if used < DEPTH:
        blocks.append(jnp.zeros((DEPTH - used, n), jnp.bfloat16))
    return jnp.concatenate(blocks, axis=0)


def inverse_factor(gram):
    k = gram.shape[0]
    row = lax.broadcasted_iota(jnp.int32, (k, k), 0)
    col = lax.broadcasted_iota(jnp.int32, (k, k), 1)
    eye = jnp.where(row == col, 1.0, 0.0)
    pad = jnp.zeros((k, LANES - 2 * k), jnp.float32)
    work = jnp.concatenate([gram, eye, pad], axis=1)
    below = lax.broadcasted_iota(jnp.int32, (k, LANES), 0)
    wide = lambda part, rows: jnp.broadcast_to(part, (rows, LANES))
    for step in range(0, k, 2):
        upper, lower = work[step : step + 1, :], work[step + 1 : step + 2, :]
        first, second = wide(work[:, step : step + 1], k), wide(work[:, step + 1 : step + 2], k)
        pivot, right = wide(upper[:, step : step + 1], 1), wide(upper[:, step + 1 : step + 2], 1)
        left, corner = wide(lower[:, step : step + 1], 1), wide(lower[:, step + 1 : step + 2], 1)
        inverse = 1.0 / pivot
        ratio = right * inverse
        upper = upper * inverse
        lower = (lower - left * upper) * (1.0 / (corner - left * ratio))
        work = (
            work
            - jnp.where(below > step, first, 0.0) * upper
            - jnp.where(below > step + 1, second - first * ratio, 0.0) * lower
        )
    diagonal = jnp.sum(work[:, :k] * eye, axis=1, keepdims=True)
    return work[:, k : 2 * k] * lax.rsqrt(diagonal)


def grid_x(C):
    size = 1
    while size * size < C:
        size *= 2
    return size


def nearest_first(X, Y):
    hops = lambda d, size: min(d, size - d)
    steps = [(hops(dy, Y) + hops(dx, X), dy * X + dx) for dy in range(Y) for dx in range(X)]
    return [step for _, step in sorted(steps)]


def chosen(i, values):
    result = values[0]
    for k, value in enumerate(values):
        result = jnp.where(i == k, value, result)
    return result


def pack(square):
    return jnp.concatenate([square[8 * i : 8 * i + 8, :] for i in range(4)], axis=1)


def unpack(flat):
    return jnp.concatenate([flat[:, 32 * i : 32 * i + 32] for i in range(4)], axis=0)


def kernel(
    R, C, n, points_ref, search_ref, applied_ref, gram_a_ref, gram_b_ref, q_ref,
    src_pts, tgt_pts, tgt_lift, tile, deg, deg_in, scal, outp,
    along_x, along_y, middle_x, middle_y, last_x, last_y,
    a_part, a_in, a_piece, a_in2, a_res,
    b_part, b_in, b_piece, b_in2, b_res,
    x_part, x_in, x_piece, x_in2, image, src_lift, local_b_ref,
    ssem, rsem,
):
    r = lax.axis_index("row")
    c = lax.axis_index("col")
    total = R * C * n
    SINGLY = {TGT: C, SRC: R // 2, SRC2: R // 2, SCAL: R // 2}
    rate = (2.0 / points_ref.shape[0]) * math.log2(math.e)

    def along_row(d):
        return lax.rem(r + d, R)

    def along_col(d):
        return lax.rem(c + d, C)

    def arrived(phase, slot):
        if phase not in SINGLY:
            return rsem.at[phase]
        first = PHASES + sum(SINGLY[p] for p in SINGLY if p < phase)
        return rsem.at[first + slot]

    def row_copy(phase, src, dst, peer, slot):
        return pltpu.make_async_remote_copy(
            src_ref=src, dst_ref=dst, send_sem=ssem.at[phase], recv_sem=arrived(phase, slot),
            device_id=(peer, c), device_id_type=MESH,
        )

    def col_copy(phase, src, dst, peer, slot):
        return pltpu.make_async_remote_copy(
            src_ref=src, dst_ref=dst, send_sem=ssem.at[phase], recv_sem=arrived(phase, slot),
            device_id=(r, peer), device_id_type=MESH,
        )

    open_ends = {}

    def await_blocks(copy, phase, buffer, count, what):
        blocks = buffer.at[pl.ds(0, count)]
        whole = copy(phase, blocks, blocks, 0, 0)
        if what == "recv":
            whole.wait_recv()
        else:
            whole.wait_send()

    def every(copy, me, size, phase, src_of, dst, what):
        def body(d, _):
            peer = lax.rem(me + d, size)
            copy(phase, src_of(peer), dst.at[me], peer, me).start()
            return 0

        if what == "start":
            for end in ("recv", "send"):
                open_ends[phase, end] = functools.partial(
                    every, copy, me, size, phase, src_of, dst, end
                )
            lax.fori_loop(1, size, body, 0)
        else:
            del open_ends[phase, what]
            await_blocks(copy, phase, dst, size - 1, what)

    row_all = functools.partial(every, row_copy, r, R)
    col_all = functools.partial(every, col_copy, c, C)

    Z = R // 2
    z0, core0 = r // 2, lax.rem(r, 2)
    partner = z0 * 2 + 1 - core0
    X = grid_x(C)
    Y = C // X
    y, x = c // X, lax.rem(c, X)
    split = search_ref.shape[0] // 2
    near = min(NEAR, Z)

    def nearest(i):
        half = (i + 1) // 2
        return lax.rem(z0 + jnp.where(lax.rem(i, 2) == 1, half, Z - half), Z)

    class Spread:
        def __init__(self, direct, handed, buffer):
            self.direct, self.handed, self.buffer = direct, handed, buffer

        def direct_copy(self, src, peer, slot):
            return pltpu.make_async_remote_copy(
                src_ref=src, dst_ref=self.buffer.at[slot], send_sem=ssem.at[self.direct],
                recv_sem=arrived(self.direct, slot // 2), device_id=(peer, c), device_id_type=MESH,
            )

        def handed_copy(self, src, slot):
            return pltpu.make_async_remote_copy(
                src_ref=src, dst_ref=self.buffer.at[slot], send_sem=ssem.at[self.handed],
                recv_sem=arrived(self.handed, slot // 2), device_id=(partner, c), device_id_type=MESH,
            )

        def start(self, src):
            self.src = src

            def body(i, _):
                self.direct_copy(src, nearest(i) * 2 + core0, r).start()
                return 0

            self.handed_copy(src, r).start()
            lax.fori_loop(1, Z, body, 0)
            open_ends[self.direct, "send"] = self.sent

        def take(self, i):
            slot = nearest(i) * 2 + core0

            def step():
                self.direct_copy(self.src, slot, slot).wait_recv()
                self.handed_copy(self.buffer.at[slot], slot).start()

            step() if isinstance(i, int) else pl.when(i > 0)(step)

            return slot

        def take_handed(self, i):
            slot = nearest(i) * 2 + 1 - core0
            self.handed_copy(self.src, slot).wait_recv()
            return slot

        def take_all_handed(self):
            await_blocks(row_copy, self.handed, self.buffer, Z, "recv")

        def sent(self):
            await_blocks(row_copy, self.direct, self.buffer, Z - 1, "send")
            await_blocks(row_copy, self.handed, self.buffer, Z, "send")

    def drain():
        for end in list(open_ends.values()):
            end()

    barrier = pltpu.get_barrier_semaphore()

    def greet_row(d, _):
        pl.semaphore_signal(barrier, inc=1, device_id=(along_row(d), c), device_id_type=MESH)
        return 0

    def greet_col(d, _):
        pl.semaphore_signal(barrier, inc=1, device_id=(r, along_col(d)), device_id_type=MESH)
        return 0

    lax.fori_loop(1, R, greet_row, 0)
    lax.fori_loop(1, C, greet_col, 0)
    search = search_ref[...]
    local_b_ref[...] = contract(search, search, ((1,), (1,)))
    src_pts[r] = points_ref[...]
    tgt_pts[c] = points_ref[...]
    pl.semaphore_wait(barrier, R + C - 2)

    my_points = lambda peer: points_ref
    sources = Spread(SRC, SRC2, src_pts)
    sources.start(points_ref)
    col_all(TGT, my_points, tgt_pts, "start")

    rows = 96
    piece = LANES // C

    def stage_square(part, square):
        wide = jnp.concatenate([square, jnp.zeros((rows, LANES - rows), jnp.float32)], axis=1)
        for i in range(C):
            if (i + 1) * piece <= rows:
                part[i] = wide[i * piece : (i + 1) * piece]
            else:
                live = max(0, rows - i * piece)
                rest = jnp.zeros((piece - live, LANES), jnp.float32)
                part[i] = jnp.concatenate([wide[i * piece : i * piece + live], rest], axis=0) if live else rest

    def round1(phase, part, inbox):
        col_all(phase, lambda peer: part.at[peer], inbox, "start")
        inbox[c] = part[c]

    def round2(phase, part, inbox, piece_ref, inbox2):
        col_all(phase, lambda peer: part.at[peer], inbox, "recv")
        value = inbox[0]
        for i in range(1, C):
            value = value + inbox[i]
        piece_ref[0] = value
        row_all(phase + 1, lambda peer: piece_ref.at[0], inbox2, "start")
        inbox2[r] = value

    def round3(phase, piece_ref, inbox2, result):
        row_all(phase + 1, lambda peer: piece_ref.at[0], inbox2, "recv")
        value = inbox2[0]
        for i in range(1, R):
            value = value + inbox2[i]
        piece_ref[1] = value * (1.0 / total)
        col_all(phase + 2, lambda peer: piece_ref.at[1], result, "start")
        result[c] = value * (1.0 / total)

    def finish(phase, piece_ref, result):
        col_all(phase + 2, lambda peer: piece_ref.at[1], result, "recv")
        square = jnp.concatenate([result[i] for i in range(C)], axis=0)
        return square[:rows, :rows]

    def small_start(phase, squares, part, inbox):
        flat = jnp.concatenate([pack(square) for square in squares], axis=0)
        part[0] = flat
        inbox[r] = flat
        row_all(phase, lambda peer: part.at[0], inbox, "start")

    def small_turn(phase, part, inbox, piece_ref, inbox2):
        row_all(phase, lambda peer: part.at[0], inbox, "recv")
        value = inbox[0]
        for i in range(1, R):
            value = value + inbox[i]
        piece_ref[0] = value
        inbox2[c] = value
        col_all(phase + 1, lambda peer: piece_ref.at[0], inbox2, "start")

    def small_finish(phase, piece_ref, inbox2, count):
        col_all(phase + 1, lambda peer: piece_ref.at[0], inbox2, "recv")
        value = inbox2[0]
        for i in range(1, C):
            value = value + inbox2[i]
        value = value * (1.0 / total)
        return [unpack(value[8 * i : 8 * i + 8]) for i in range(count)]


    def affinities(exponent, slots, at, width):
        affinity = jnp.exp2(exponent)
        rows_in = n * len(slots)
        deg[:, at] += jnp.sum(affinity.reshape(rows_in // 8, 8, width), axis=0)
        low = affinity.astype(jnp.bfloat16)
        for i, slot in enumerate(slots):
            tile[pl.ds(pl.multiple_of(slot * n, n), n), at] = low[i * n : (i + 1) * n]

    def cross(lifted_sources, lifted_targets):
        return lax.dot_general(
            lifted_sources, lifted_targets, (((0,), (0,)), ((), ())),
            preferred_element_type=jnp.float32,
        )

    deg[...] = jnp.zeros_like(deg)
    early = [r, partner]
    src_lift[:, 0:n] = lifted(points_ref[...], rate, True)
    sources.take_handed(0)
    src_lift[:, n : 2 * n] = lifted(src_pts[partner], rate, True)
    for i in range(1, near):
        early.append(sources.take(i))
        src_lift[:, (i + 1) * n : (i + 2) * n] = lifted(src_pts[early[-1]], rate, True)

    def early_cells(i, _):
        away = chosen(i, nearest_first(X, Y))
        peer = lax.rem(y + away // X, Y) * X + lax.rem(x + lax.rem(away, X), X)

        @pl.when(i > 0)
        def _():
            col_copy(TGT, points_ref, tgt_pts.at[peer], peer, peer).wait_recv()

        at = pl.ds(pl.multiple_of(peer * n, n), n)
        targets = lifted(tgt_pts[peer], rate, False)
        tgt_lift[:, at] = targets
        affinities(cross(src_lift[...], targets), early, at, n)
        return 0

    lax.fori_loop(0, C, early_cells, 0)
    del open_ends[TGT, "recv"]
    stage_square(b_part, local_b_ref[...])
    round1(B1, b_part, b_in)

    def block_rows(slots):
        lifts = [lifted(src_pts[slot], rate, True) for slot in slots]
        affinities(
            cross(jnp.concatenate(lifts, axis=1), tgt_lift[...]), slots, slice(None), C * n
        )
        return 0

    lax.fori_loop(
        near, Z, lambda i, _: block_rows([sources.take(i), sources.take_handed(i - near + 1)]), 0
    )
    block_rows([sources.take_handed(i) for i in range(Z - near + 1, Z)])

    window = lambda peer: deg.at[:, pl.ds(pl.multiple_of(peer * n, n), n)]
    col_all(DEG, window, deg_in, "start")
    deg_in[c] = deg[:, pl.ds(pl.multiple_of(c * n, n), n)]
    round2(B1, b_part, b_in, b_piece, b_in2)
    col_all(DEG, window, deg_in, "recv")
    sums = deg_in[0]
    for i in range(1, C):
        sums = sums + deg_in[i]
    degrees = jnp.sum(sums, axis=0, keepdims=True)
    root = lax.rsqrt(degrees)
    root = root * (1.5 - 0.5 * degrees * root * root)
    scal[r] = (search_ref[...] * root).astype(jnp.bfloat16)
    blocks = Spread(SCAL, SCAL2, scal)
    blocks.start(scal.at[r])

    def near_images(i, _):
        slot = blocks.take(i)
        value = jnp.dot(
            scal[slot], tile[pl.ds(pl.multiple_of(slot * n, n), n), :],
            preferred_element_type=jnp.float32,
        )

        @pl.when(i == 0)
        def _():
            image[...] = value

        @pl.when(i > 0)
        def _():
            image[...] += value

        return 0

    lax.fori_loop(0, Z, near_images, 0)

    round3(B1, b_piece, b_in2, b_res)
    blocks.take_all_handed()
    pairs = C // 2
    pair0 = c // 2

    def images(j, _):
        pair = lax.rem(pair0 + 1 + j, pairs)
        at = pl.ds(pl.multiple_of(pair * (2 * n), 2 * n), 2 * n)
        value = image[:, at]
        for i in range(Z):
            slot = i * 2 + 1 - core0
            value = value + jnp.dot(
                scal[slot], tile[pl.ds(pl.multiple_of(slot * n, n), n), at],
                preferred_element_type=jnp.float32,
            )
        for half in range(2):
            block = pair * 2 + half
            by, bx = block // X, lax.rem(block, X)
            mine = value[:, half * n : (half + 1) * n]
            outp[block, 0] = mine[:split]
            outp[block, 1] = mine[split:]

            @pl.when(bx != x)
            def _():
                col_copy(O1, outp.at[block, 0], along_x.at[x * Y + by], y * X + bx, 0).start()

            @pl.when(bx == x)
            def _():
                along_x[x * Y + by] = mine[:split]

            @pl.when(by != y)
            def _():
                col_copy(O2, outp.at[block, 1], along_y.at[y * X + bx], by * X + x, 0).start()

            @pl.when(by == y)
            def _():
                along_y[y * X + bx] = mine[split:]

        return 0

    lax.fori_loop(0, pairs, images, 0)

    def second(phase, inbox, count, size, me, device, middle, last, phase_out):
        if count > 1:
            await_blocks(col_copy, phase, inbox, (count - 1) * size, "recv")

        def body(i, _):
            at = lax.rem(me + 1 + i, size)
            value = inbox[at]
            for k in range(1, count):
                value = value + inbox[k * size + at]

            @pl.when(at != me)
            def _():
                middle[at] = value
                col_copy(phase_out, middle.at[at], last.at[me], device(at), 0).start()

            @pl.when(at == me)
            def _():
                last[me] = value

            return 0

        lax.fori_loop(0, size, body, 0)

    gram_b = finish(B1, b_piece, b_res)
    gram_b_ref[...] = gram_b
    factor = inverse_factor(gram_b[:NEV, :NEV])

    second(O1, along_x, X, Y, y, lambda at: at * X + x, middle_y, last_y, O3)
    second(O2, along_y, Y, X, x, lambda at: y * X + at, middle_x, last_x, O4)

    def ends(what):
        for phase, buffer, count in (
            (O1, along_x, (X - 1) * Y), (O2, along_y, (Y - 1) * X), (O3, last_y, Y - 1), (O4, last_x, X - 1),
        ):
            if count and not (what == "recv" and phase in (O1, O2)):
                await_blocks(col_copy, phase, buffer, count, what)

    ends("recv")
    open_ends[O1, "send"] = functools.partial(ends, "send")
    upper, lower = last_y[0], last_x[0]
    for i in range(1, Y):
        upper = upper + last_y[i]
    for i in range(1, X):
        lower = lower + last_x[i]
    sums = jnp.concatenate([upper, lower], axis=0)
    applied = sums * root
    applied_ref[...] = applied

    both = jnp.concatenate([search_ref[...], applied[:NEV]], axis=0)
    products = contract(both, applied, ((1,), (1,)))
    small_start(X1, [products[:NEV, :NEV], products[rows:, :NEV]], x_part, x_in)
    stage_square(a_part, products[:rows])
    round1(A1, a_part, a_in)
    small_turn(X1, x_part, x_in, x_piece, x_in2)
    round2(A1, a_part, a_in, a_piece, a_in2)
    solved = contract(factor, contract(factor, search_ref[:NEV, :], ((1,), (0,))), ((0,), (0,)))
    leading, images_gram = small_finish(X1, x_piece, x_in2, 2)
    projected = contract(factor, leading, ((1,), (0,)))
    residual_gram = images_gram - contract(projected, projected, ((0,), (0,)))
    round3(A1, a_piece, a_in2, a_res)
    residual = applied[:NEV] - contract(leading, solved, ((0,), (0,)))
    q_ref[...] = contract(inverse_factor(residual_gram), residual, ((1,), (0,)))
    gram_a_ref[...] = finish(A1, a_piece, a_res)
    drain()


def per_device(R, C, points, search):
    dim, n = points.shape
    rows = search.shape[0]
    f32 = jnp.float32
    piece = LANES // C
    square = lambda: [
        pltpu.VMEM((C, piece, LANES), f32),
        pltpu.VMEM((C, piece, LANES), f32),
        pltpu.VMEM((2, piece, LANES), f32),
        pltpu.VMEM((R, piece, LANES), f32),
        pltpu.VMEM((C, piece, LANES), f32),
    ]
    small = lambda: [
        pltpu.VMEM((1, 16, LANES), f32),
        pltpu.VMEM((R, 16, LANES), f32),
        pltpu.VMEM((1, 16, LANES), f32),
        pltpu.VMEM((C, 16, LANES), f32),
    ]
    vmem = pl.BlockSpec(memory_space=pltpu.VMEM)
    X = grid_x(C)
    singly = C + 3 * (R // 2)
    return pl.pallas_call(
        functools.partial(kernel, R, C, n),
        out_shape=(
            jax.ShapeDtypeStruct((rows, n), f32),
            jax.ShapeDtypeStruct((rows, rows), f32),
            jax.ShapeDtypeStruct((rows, rows), f32),
            jax.ShapeDtypeStruct((NEV, n), f32),
        ),
        in_specs=[vmem, vmem],
        out_specs=(vmem, vmem, vmem, vmem),
        scratch_shapes=[
            pltpu.VMEM((R, dim, n), f32),
            pltpu.VMEM((C, dim, n), f32),
            pltpu.VMEM((DEPTH, C * n), jnp.bfloat16),
            pltpu.VMEM((R * n, C * n), jnp.bfloat16),
            pltpu.VMEM((8, C * n), f32),
            pltpu.VMEM((C, 8, n), f32),
            pltpu.VMEM((R, rows, n), jnp.bfloat16),
            pltpu.VMEM((C, 2, rows // 2, n), f32),
            pltpu.VMEM((C, rows // 2, n), f32),
            pltpu.VMEM((C, rows // 2, n), f32),
            pltpu.VMEM((X, rows // 2, n), f32),
            pltpu.VMEM((C // X, rows // 2, n), f32),
            pltpu.VMEM((X, rows // 2, n), f32),
            pltpu.VMEM((C // X, rows // 2, n), f32),
            *square(),
            *square(),
            *small(),
            pltpu.VMEM((rows, C * n), f32),
            pltpu.VMEM((DEPTH, (min(NEAR, R // 2) + 1) * n), jnp.bfloat16),
            pltpu.VMEM((rows, rows), f32),
            pltpu.SemaphoreType.DMA((PHASES,)),
            pltpu.SemaphoreType.DMA((PHASES + singly,)),
        ],
        compiler_params=pltpu.CompilerParams(
            collective_id=0, has_side_effects=True, vmem_limit_bytes=60 << 20
        ),
    )(points, search)


def solution(mesh):
    placed = (P(None, ("row", "col")), P(None, ("row", "col")))
    return jax.shard_map(
        functools.partial(per_device, mesh.shape["row"], mesh.shape["col"]),
        mesh=mesh,
        in_specs=placed,
        out_specs=(P(None, ("row", "col")), P(), P(), P(None, ("row", "col"))),
        check_vma=False,
    )
```
